32 devices in a mesh: days: 2 (over y), sensor: 4 (over z), band: 2 (over x), win: 2 (over core).
Axes of the slice: x: 2, y: 2, z: 4, core: 2. Of those that a mesh axis runs over, the one named last changes fastest.
Arguments:
- records: bfloat16 [192, 32, 2048], P('days', 'sensor', ('band', 'win')), parts along dimension 0, may hold values from -6 to 6
- alive: int32 [192, 32], P('days', 'sensor'), parts along dimension 0, may hold values 0 or 1
Outputs:
- correlation: float32 [64, 32, 601], P(('days', 'sensor'), ('band', 'win')), parts along dimension 0
The draws below stay inside these ranges and needn't reach their ends.
There are 2 independent parts, one for each index of `days`. The reference program is written for one: setup_inputs(seed, part) draws one part's arguments, and reference() takes and returns one part's arrays. A program takes and returns all parts, laid end to end along the dimension named above; each array names one. Nothing has to cross between parts.
All inputs are finite; a program needn't handle non-finite values. No bound on the sum of `alive` on one device may be relied on, other than what follows from the above.
Results may differ from the reference program's by a relative error of at most 0.0027.
Values may be sent and summed in bfloat16 or wider, within the bound.
A program may use at most 64 MiB of HBM per device.

```python
import math
import jax
import jax.numpy as jnp
from jax import lax

SAMPLES = 2048
MAXLAG = 300
WINDOWS = 96
SENS_DEV = 8
SENSORS = 32
N_SENSOR = 4


def touch_ends(drawn, key, smallest, high):
    longest = drawn.shape.index(max(drawn.shape))
    spots = []
    for shift in (0, 1):
        where = [jax.random.randint(jax.random.fold_in(key, axis), (), 0, length) for axis, length in enumerate(drawn.shape)]
        where[longest] = (where[longest] + shift) % drawn.shape[longest]
        spots.append(tuple(where))
    return drawn.at[spots[0]].set(smallest).at[spots[1]].set(high)


def level_of(rng, extent, cuts, smallest, high):
    def one(position, parts):
        draws = jax.random.uniform(jax.random.fold_in(jax.random.fold_in(rng, 6), position), (parts,), jnp.float32, smallest / len(cuts), high / len(cuts))
        return jnp.repeat(jnp.exp(draws), extent[position] // parts).reshape((-1,) + (1,) * (len(extent) - position - 1))

    gain = one(*cuts[0])
    for cut in cuts[1:]:
        gain = gain * one(*cut)
    return gain


def normal_values(stream_key, shape, scale, most, split=(), kind=jnp.bfloat16):
    result = scale * jax.random.normal(stream_key, shape, jnp.float32)
    if split:
        result = result * level_of(stream_key, shape, split, -0.22, 0.18)
    return jnp.clip(result, -most, most).astype(kind)


def setup_inputs(seed: int = 0, part: int = 0) -> dict:
    arg_keys = jax.random.split(jax.random.key(seed), 3)
    own_keys = jax.random.split(jax.random.fold_in(arg_keys[2], part), 3)
    records = normal_values(own_keys[0], (WINDOWS, SENSORS, SAMPLES), 1.0, 6.0, ((1, 4), (2, 4)))
    alive = touch_ends((jax.random.randint(own_keys[1], (WINDOWS, SENSORS), 0, 8) < 7).astype(jnp.int32), jax.random.fold_in(own_keys[1], 1), 0, 1)
    return {"records": records, "alive": alive}


WHITEN_FLOOR = 0.5

def spectrum_table(samples, bin_count):
    time_index = lax.broadcasted_iota(jnp.int32, (samples, bin_count), 0)
    freq_index = lax.broadcasted_iota(jnp.int32, (samples, bin_count), 1)
    phase_angle = (time_index * freq_index % samples).astype(jnp.float32) * (2.0 * math.pi / samples)
    basis_table = jnp.concatenate([jnp.cos(phase_angle), -jnp.sin(phase_angle)], axis=1) / math.sqrt(samples)
    return basis_table.astype(jnp.bfloat16)

def lag_table(samples, bin_count, maxlag):
    lag_count = 2 * maxlag + 1
    freq_index = lax.broadcasted_iota(jnp.int32, (bin_count, lag_count), 0)
    shifts = lax.broadcasted_iota(jnp.int32, (bin_count, lag_count), 1) - maxlag
    phase_angle = (freq_index * shifts % samples).astype(jnp.float32) * (2.0 * math.pi / samples)
    weight = jnp.where(freq_index == 0, 1.0, 2.0).astype(jnp.float32) / (2.0 * math.sqrt(bin_count))
    basis_table = jnp.concatenate([weight * jnp.cos(phase_angle), -weight * jnp.sin(phase_angle)], axis=0)
    return basis_table.astype(jnp.bfloat16)

def reference(records, alive):
    bin_count = SAMPLES // 2
    dft_basis = spectrum_table(SAMPLES, bin_count)
    spectra = jnp.dot(records.reshape(-1, SAMPLES), dft_basis, preferred_element_type=jnp.float32)
    spectra = spectra.reshape(WINDOWS, SENSORS, 2, bin_count)
    power_sum = spectra[:, :, 0] * spectra[:, :, 0] + spectra[:, :, 1] * spectra[:, :, 1]
    whitened = (spectra * lax.rsqrt(power_sum + WHITEN_FLOOR)[:, :, None, :]).astype(jnp.bfloat16)
    whitened = whitened * alive.astype(jnp.bfloat16)[:, :, None, None]
    lag_basis = lag_table(SAMPLES, bin_count, MAXLAG)
    window_scale = 1.0 / math.sqrt(WINDOWS)
    whole_spec = whitened.astype(jnp.float32)

    def block_lags(begin_at):
        local_spec = lax.dynamic_slice_in_dim(whole_spec, begin_at, SENS_DEV, 1)
        products = jnp.einsum('wicf,wjdf->ijcdf', local_spec, whole_spec)
        real_part = products[:, :, 0, 0] + products[:, :, 1, 1]
        imag_part = products[:, :, 1, 0] - products[:, :, 0, 1]
        stacked = (jnp.stack([real_part, imag_part], axis=2) * window_scale).astype(jnp.bfloat16)
        flattened = stacked.reshape(SENS_DEV * SENSORS, 2 * bin_count)
        lagged = jnp.dot(flattened, lag_basis, preferred_element_type=jnp.float32)
        return lagged.reshape(SENS_DEV, SENSORS, 2 * MAXLAG + 1)
    starts = (jnp.arange(N_SENSOR) * SENS_DEV).astype(jnp.int32)
    blocks = lax.map(block_lags, starts)
    return blocks.reshape(SENSORS, SENSORS, 2 * MAXLAG + 1)
```

```python
import functools
import math

import jax
import jax.numpy as jnp
import ml_dtypes
import numpy as np
from jax import lax
from jax.experimental import pallas as pl
from jax.experimental.pallas import tpu as pltpu
from jax.sharding import PartitionSpec as P

MAXLAG = 300
WHITEN_FLOOR = 0.5
LANES = 128
UNROLL = 2
BATCHES = 3
SPLITS = 2
ROW_AXES = ("band", "win")
MESH = pl.DeviceIdType.MESH


def spectrum_table(samples, bin_count):
    time_index = np.arange(samples, dtype=np.int64)[:, None]
    freq_index = np.arange(bin_count, dtype=np.int64)[None, :]
    phase_angle = (time_index * freq_index % samples).astype(np.float32) * np.float32(
        2.0 * math.pi / samples
    )
    phase_angle = phase_angle.astype(np.float64)
    table = np.stack([np.cos(phase_angle), -np.sin(phase_angle)], axis=1)
    table = table.astype(np.float32) / np.float32(math.sqrt(samples))
    return table.astype(ml_dtypes.bfloat16)


def lag_table(samples, bin_count, maxlag):
    lag_count = 2 * maxlag + 1
    freq_index = np.arange(bin_count, dtype=np.int64)[:, None]
    shifts = np.arange(lag_count, dtype=np.int64)[None, :] - maxlag
    phase_angle = (freq_index * shifts % samples).astype(np.float32) * np.float32(
        2.0 * math.pi / samples
    )
    phase_angle = phase_angle.astype(np.float64)
    weight = np.where(freq_index == 0, 1.0, 2.0).astype(np.float32) / np.float32(
        2.0 * math.sqrt(bin_count)
    )
    table = np.stack([np.cos(phase_angle), -np.sin(phase_angle)], axis=0)
    table = weight[None] * table.astype(np.float32)
    return table.astype(ml_dtypes.bfloat16)


def kernel(
    sensor_n, band_n, win_n, item_count,
    records, alive_hbm, basis_hbm, lag_hbm, out,
    alive, basis, lag, rows_in, outgoing, spread, wide, turned, totals, stacked, sending, homed,
    table_sem, own_sem, near_sem, far_sem, send1, recv1, send2, recv2, send3, recv3,
):
    z, b, c = lax.axis_index("sensor"), lax.axis_index("band"), lax.axis_index("win")
    groups = band_n * win_n
    g = b * win_n + c
    me = z * groups + g
    rows, samples = rows_in.shape
    part = samples // groups
    shard = alive.shape[0]
    half = LANES // 2
    local_items = item_count // groups

    offsets = [
        (dz, db, dc) for dz in range(sensor_n) for db in range(band_n) for dc in range(win_n)
    ]

    def peer(dz, db, dc):
        return (
            lax.rem(z + dz, sensor_n),
            lax.rem(b + db, band_n),
            lax.rem(c + dc, win_n),
        )

    def ident(place):
        return {"sensor": place[0], "band": place[1], "win": place[2]}

    alive_copy = pltpu.make_async_copy(alive_hbm, alive, table_sem.at[2])
    alive_copy.start()
    basis_copy = pltpu.make_async_copy(basis_hbm, basis, table_sem.at[0])
    lag_copy = pltpu.make_async_copy(lag_hbm, lag, table_sem.at[1])

    def mine_of(group, start, count):
        return records.at[pl.ds(pl.multiple_of(group * rows + start, 8), count)]

    def columns_of(group, start, count):
        columns = pl.ds(pl.multiple_of(group * part, LANES), part)
        return rows_in.at[start : start + count, columns]

    own_copy = pltpu.make_async_copy(mine_of(g, 0, rows), columns_of(g, 0, rows), own_sem.at[0])
    own_copy.start()

    mate = ident(peer(0, 0, 1))
    first, second = c == 0, c == 1
    barrier = pltpu.get_barrier_semaphore()
    for off in offsets[1:]:
        place = peer(*off)

        @pl.when(place[2] == (0 if off[0] == 0 else 1))
        def _(place=place):
            pl.semaphore_signal(barrier, inc=1, device_id=ident(place), device_id_type=MESH)

    basis_copy.start()

    @pl.when(first)
    def _():
        pl.semaphore_wait(barrier, groups - 1)
        pl.semaphore_signal(near_sem, inc=1, device_id=mate, device_id_type=MESH)

    @pl.when(second)
    def _():
        pl.semaphore_wait(near_sem, 1)

    step_rows = rows // BATCHES
    copies1 = {}
    for turn in range(BATCHES):
        for db in reversed(range(band_n)):
            for dc in range(win_n):
                if (db, dc) == (0, 0):
                    continue
                slot = turn * groups + db * win_n + dc
                place = peer(0, db, dc)
                copy = pltpu.make_async_remote_copy(
                    src_ref=mine_of(place[1] * win_n + place[2], turn * step_rows, step_rows),
                    dst_ref=columns_of(g, turn * step_rows, step_rows),
                    send_sem=send1.at[slot],
                    recv_sem=recv1.at[slot],
                    device_id=ident(place),
                    device_id_type=MESH,
                )
                copy.start()
                copies1[turn, db, dc] = copy
    lag_copy.start()

    alive_copy.wait()
    row_item = lax.broadcasted_iota(jnp.int32, (rows, item_count), 0) // shard
    item = lax.broadcasted_iota(jnp.int32, (rows, item_count), 1)
    pick = jnp.where(row_item + g * local_items == item, 1.0, 0.0)
    spread_alive = lax.dot_general(
        pick.astype(jnp.bfloat16),
        alive[...].astype(jnp.float32).astype(jnp.bfloat16),
        (((1,), (1,)), ((), ())),
        preferred_element_type=jnp.float32,
    )
    row_sensor = lax.rem(lax.broadcasted_iota(jnp.int32, (rows, shard), 0), shard)
    column = lax.broadcasted_iota(jnp.int32, (rows, shard), 1)
    usable = jnp.sum(
        jnp.where(row_sensor == column, spread_alive, 0.0), axis=1, keepdims=True
    )

    own_copy.wait()
    basis_copy.wait()

    @pl.when(second)
    def _():
        pl.semaphore_wait(barrier, (sensor_n - 1) * groups)
        pl.semaphore_signal(far_sem, inc=1, device_id=mate, device_id_type=MESH)

    @pl.when(first)
    def _():
        pl.semaphore_wait(far_sem, 1)

    copies2 = {}
    order = [(dz, db) for db in range(band_n) for dz in range(sensor_n)]
    order = order[1:sensor_n] + order[:1] + order[sensor_n:]
    for turn in range(BATCHES):
        lines = slice(turn * step_rows, (turn + 1) * step_rows)
        for (at, _, _), copy in copies1.items():
            if at == turn:
                copy.wait_recv()
        for step, (dz, db) in enumerate(order):
            place_z, place_b, _ = peer(dz, db, 0)
            spectra = jnp.dot(
                rows_in[lines, :],
                basis[place_z * band_n + place_b],
                preferred_element_type=jnp.float32,
            )
            for core in range(win_n):
                piece = spectra[:, core * LANES : (core + 1) * LANES]
                square = piece * piece
                power = square + pltpu.roll(square, half, 1)
                white = piece * (lax.rsqrt(power + WHITEN_FLOOR) * usable[lines])
                outgoing[turn, step, core] = white.astype(jnp.bfloat16)
            for dc in range(win_n):
                place = peer(dz, db, dc)
                if (dz, db, dc) == (0, 0, 0):
                    spread[me, lines, :] = outgoing[turn, step, c]
                    continue
                slot = ((turn * sensor_n + dz) * band_n + db) * win_n + dc
                copy = pltpu.make_async_remote_copy(
                    src_ref=outgoing.at[turn, step, place[2]],
                    dst_ref=spread.at[me, lines],
                    send_sem=send2.at[slot],
                    recv_sem=recv2.at[slot],
                    device_id=ident(place),
                    device_id_type=MESH,
                )
                copy.start()
                copies2[turn, dz, db, dc] = copy

    lane = lax.broadcasted_iota(jnp.int32, (shard, LANES), 1)
    window_scale = 1.0 / math.sqrt(item_count)
    near = [(db, dc) for db in range(band_n) for dc in range(win_n)]
    wave = len(near) // SPLITS
    waves = [
        (turn, near[at : at + wave])
        for turn in range(BATCHES)
        for at in range(0, len(near), wave)
    ]
    step_items = step_rows // shard
    for stage, (turn, sources) in enumerate(waves):
        lines = slice(turn * step_rows, (turn + 1) * step_rows)
        for db, dc in sources:
            for dz in range(sensor_n):
                if (dz, db, dc) != (0, 0, 0):
                    copies2[turn, dz, db, dc].wait_recv()
        for k, (db, dc) in enumerate(sources):
            source_g = lax.rem(b + band_n - db, band_n) * win_n + lax.rem(c + win_n - dc, win_n)
            items = slice(k * step_items, (k + 1) * step_items)
            for source_z in range(sensor_n):
                block = spread[source_z * groups + source_g, lines, :].astype(jnp.float32)
                wide[source_z, items] = block.reshape(step_items, shard, LANES)
                turned[source_z, items] = pltpu.roll(block, half, 1).reshape(
                    step_items, shard, LANES
                )

        for first_z in range(sensor_n):
            seconds = list(range(first_z, sensor_n))
            batch = 4 if len(seconds) > 2 else 8
            for begin in range(0, shard, batch):
                places = [
                    (second_z, part, begin + k)
                    for second_z in seconds
                    for k in range(batch)
                    for part in range(2)
                ]

                def add(w, sums, first_z=first_z, begin=begin, batch=batch, places=places):
                    left = [
                        jnp.broadcast_to(wide[first_z, w, s : s + 1, :], (shard, LANES))
                        for s in range(begin, begin + batch)
                    ]
                    right = {
                        (z2, part): (turned if part else wide)[z2, w]
                        for z2 in range(first_z, sensor_n)
                        for part in range(2)
                    }
                    return tuple(
                        total + left[s - begin] * right[z2, part]
                        for total, (z2, part, s) in zip(sums, places, strict=True)
                    )

                if stage == 0:
                    start = (jnp.zeros((shard, LANES), jnp.float32),) * len(places)
                else:
                    start = tuple(
                        totals[first_z * sensor_n + z2, part, s] for z2, part, s in places
                    )
                sums = lax.fori_loop(
                    0, wave * step_items, add, start, unroll=UNROLL
                )
                if stage < len(waves) - 1:
                    for total, (z2, part, s) in zip(sums, places, strict=True):
                        totals[first_z * sensor_n + z2, part, s] = total
                    continue
                found = dict(zip(places, sums, strict=True))
                for z2 in seconds:
                    for s in range(begin, begin + batch):
                        same, cross = found[z2, 0, s], found[z2, 1, s]
                        real = (same + pltpu.roll(same, half, 1)) * window_scale
                        imag = (cross - pltpu.roll(cross, half, 1)) * window_scale
                        stacked[first_z * groups + z2, s * shard : (s + 1) * shard, :] = jnp.where(
                            lane < half, real, imag
                        )
                        if z2 != first_z:
                            stacked[z2 * groups + first_z, pl.ds(s, shard, stride=shard), :] = (
                                jnp.where(lane < half, real, -imag)
                            )
    for copy in [*copies1.values(), *copies2.values()]:
        copy.wait_send()

    @pl.loop(0, sensor_n * groups)
    def _(i):
        sending[i] = stacked[i].astype(jnp.bfloat16)

    target = homed.at[:, pl.ds(pl.multiple_of(me * LANES, LANES), LANES)]
    copies3 = []
    for dz, db, dc in offsets:
        place = peer(dz, db, dc)
        block = sending.at[(place[0] * band_n + place[1]) * win_n + place[2]]
        slot = (dz * band_n + db) * win_n + dc
        if slot == 0:
            copy = pltpu.make_async_copy(block, target, own_sem.at[1])
        else:
            copy = pltpu.make_async_remote_copy(
                src_ref=block,
                dst_ref=target,
                send_sem=send3.at[slot],
                recv_sem=recv3.at[slot],
                device_id=ident(place),
                device_id_type=MESH,
            )
        copy.start()
        copies3.append(copy)
    lag_copy.wait()
    for copy in copies3:
        copy.wait()
    lagged = jnp.dot(homed[...], lag[...], preferred_element_type=jnp.float32)
    out[...] = lagged[:, : out.shape[1]]


def fused(sizes, records, alive):
    sensor_n, band_n, win_n = sizes
    groups = band_n * win_n
    peers = sensor_n * groups
    item_count, shard, part = records.shape
    samples = part * groups
    bin_count = samples // 2
    half = LANES // 2
    rows = item_count // groups * shard
    lag_count = 2 * MAXLAG + 1
    stage_items = item_count // (BATCHES * SPLITS)
    lag_room = -(-lag_count // LANES) * LANES
    table = spectrum_table(samples, bin_count).reshape(samples, 2, peers, half)
    table = table.transpose(0, 2, 1, 3).reshape(samples, peers // win_n, win_n * LANES)
    basis = np.ascontiguousarray(table.transpose(1, 0, 2))
    table = lag_table(samples, bin_count, MAXLAG).reshape(2, peers, half, lag_count)
    table = table.transpose(1, 0, 2, 3).reshape(2 * bin_count, lag_count)
    lag = np.zeros((2 * bin_count, lag_room), ml_dtypes.bfloat16)
    lag[:, :lag_count] = table
    vmem = pl.BlockSpec(memory_space=pltpu.VMEM)
    far = pl.BlockSpec(memory_space=pltpu.HBM)
    dma = pltpu.SemaphoreType.DMA
    result = pl.pallas_call(
        functools.partial(kernel, sensor_n, band_n, win_n, item_count),
        out_shape=jax.ShapeDtypeStruct((shard * shard, lag_count), jnp.float32),
        in_specs=[far, far, far, far],
        out_specs=vmem,
        scratch_shapes=[
            pltpu.VMEM((shard, item_count), jnp.int32),
            pltpu.VMEM(basis.shape, jnp.bfloat16),
            pltpu.VMEM(lag.shape, jnp.bfloat16),
            pltpu.VMEM((rows, samples), jnp.bfloat16),
            pltpu.VMEM((BATCHES, peers // win_n, win_n, rows // BATCHES, LANES), jnp.bfloat16),
            pltpu.VMEM((peers, rows, LANES), jnp.bfloat16),
            pltpu.VMEM((sensor_n, stage_items, shard, LANES), jnp.float32),
            pltpu.VMEM((sensor_n, stage_items, shard, LANES), jnp.float32),
            pltpu.VMEM((peers, 2, shard, shard, LANES), jnp.float32),
            pltpu.VMEM((peers, shard * shard, LANES), jnp.float32),
            pltpu.VMEM((peers, shard * shard, LANES), jnp.bfloat16),
            pltpu.VMEM((shard * shard, samples), jnp.bfloat16),
            dma((3,)),
            dma((2,)),
            pltpu.SemaphoreType.REGULAR,
            pltpu.SemaphoreType.REGULAR,
            dma((BATCHES * groups,)),
            dma((BATCHES * groups,)),
            dma((BATCHES * peers,)),
            dma((BATCHES * peers,)),
            dma((peers,)),
            dma((peers,)),
        ],
        compiler_params=pltpu.CompilerParams(
            collective_id=0, has_side_effects=True, vmem_limit_bytes=56 << 20
        ),
    )(
        records.reshape(item_count * shard, part),
        alive.T,
        jnp.asarray(basis),
        jnp.asarray(lag),
    )
    return result.reshape(shard, shard, lag_count)


def cross_block(local_spec, incoming, window_scale):
    products = jnp.einsum(
        "wicf,nwjdf->injcdf", local_spec, incoming, preferred_element_type=jnp.float32
    )
    real_part = products[:, :, :, 0, 0] + products[:, :, :, 1, 1]
    imag_part = products[:, :, :, 1, 0] - products[:, :, :, 0, 1]
    return jnp.stack([real_part, imag_part], axis=3) * window_scale


def general(records, alive):
    groups = lax.axis_size(ROW_AXES)
    sensors_count = lax.axis_size("sensor")
    shard_sensors = records.shape[1]
    samples = records.shape[2] * groups
    bin_count = samples // 2
    bins_local = bin_count // groups
    dft_basis = jnp.asarray(spectrum_table(samples, bin_count).reshape(samples, -1))
    pieces = lax.all_to_all(records, ROW_AXES, split_axis=1, concat_axis=2, tiled=True)
    item_count = pieces.shape[0]
    sample_rows = pieces.reshape(-1, samples)
    spectra = jnp.dot(sample_rows, dft_basis, preferred_element_type=jnp.float32)
    spectra = spectra.reshape(item_count, -1, 2, bin_count)
    power_sum = spectra[:, :, 0] * spectra[:, :, 0] + spectra[:, :, 1] * spectra[:, :, 1]
    whitened = (spectra * lax.rsqrt(power_sum + WHITEN_FLOOR)[:, :, None, :]).astype(jnp.bfloat16)
    spectra = lax.all_to_all(whitened, ROW_AXES, split_axis=3, concat_axis=1, tiled=True)
    spectra = spectra * alive.astype(jnp.bfloat16)[:, :, None, None]
    window_scale = 1.0 / math.sqrt(spectra.shape[0])
    spread = lax.all_to_all(spectra, "sensor", split_axis=3, concat_axis=1, tiled=True)
    every_pair = cross_block(spread, spread[None], window_scale)[:, 0]
    paired = every_pair.astype(jnp.bfloat16)
    homed = lax.all_to_all(paired, "sensor", split_axis=0, concat_axis=3, tiled=True)
    stacked = homed.reshape(shard_sensors, sensors_count, shard_sensors, 2, bins_local)
    relaid = lax.all_to_all(stacked, ROW_AXES, split_axis=1, concat_axis=4, tiled=True)
    flattened = relaid.reshape(-1, 2 * bin_count)
    lag_basis = jnp.asarray(lag_table(samples, bin_count, MAXLAG).reshape(2 * bin_count, -1))
    lagged = jnp.dot(flattened, lag_basis, preferred_element_type=jnp.float32)
    return lagged.reshape(shard_sensors, -1, 2 * MAXLAG + 1)


def body(sizes, records, alive):
    sensor_n, band_n, win_n = sizes
    groups = band_n * win_n
    item_count, shard, part = records.shape
    fits = (
        part * groups == sensor_n * groups * LANES
        and sensor_n == groups
        and win_n == 2
        and shard == 8
        and item_count % (2 * groups * BATCHES) == 0
        and part % LANES == 0
    )
    if fits:
        return fused(sizes, records, alive)
    return general(records, alive)


def solution(mesh):
    sizes = tuple(mesh.shape[name] for name in ("sensor", "band", "win"))
    return jax.shard_map(
        functools.partial(body, sizes),
        mesh=mesh,
        in_specs=(P("days", "sensor", ROW_AXES), P("days", "sensor")),
        out_specs=P(("days", "sensor"), ROW_AXES, None),
        check_vma=False,
    )
```

```python
import functools
import math

import jax
import jax.numpy as jnp
import ml_dtypes
import numpy as np
from jax import lax
from jax.experimental import pallas as pl
from jax.experimental.pallas import tpu as pltpu
from jax.sharding import PartitionSpec as P

MAXLAG = 300
WHITEN_FLOOR = 0.5
LANES = 128
UNROLL = 2
CHUNKS = (8, 8, 8)
SPLITS = (2, 2, 2)
ROW_AXES = ("band", "win")
MESH = pl.DeviceIdType.MESH


def spectrum_table(samples, bin_count):
    time_index = np.arange(samples, dtype=np.int64)[:, None]
    freq_index = np.arange(bin_count, dtype=np.int64)[None, :]
    phase_angle = (time_index * freq_index % samples).astype(np.float32) * np.float32(
        2.0 * math.pi / samples
    )
    phase_angle = phase_angle.astype(np.float64)
    table = np.stack([np.cos(phase_angle), -np.sin(phase_angle)], axis=1)
    table = table.astype(np.float32) / np.float32(math.sqrt(samples))
    return table.astype(ml_dtypes.bfloat16)


def lag_table(samples, bin_count, maxlag):
    lag_count = 2 * maxlag + 1
    freq_index = np.arange(bin_count, dtype=np.int64)[:, None]
    shifts = np.arange(lag_count, dtype=np.int64)[None, :] - maxlag
    phase_angle = (freq_index * shifts % samples).astype(np.float32) * np.float32(
        2.0 * math.pi / samples
    )
    phase_angle = phase_angle.astype(np.float64)
    weight = np.where(freq_index == 0, 1.0, 2.0).astype(np.float32) / np.float32(
        2.0 * math.sqrt(bin_count)
    )
    table = np.stack([np.cos(phase_angle), -np.sin(phase_angle)], axis=0)
    table = weight[None] * table.astype(np.float32)
    return table.astype(ml_dtypes.bfloat16)


def kernel(
    sensor_n, band_n, win_n, item_count,
    records, alive_hbm, basis_hbm, lag_hbm, out,
    alive, basis, lag, rows_in, outgoing, spread, wide, turned, totals, stacked, sending, homed,
    table_sem, own_sem, near_sem, far_sem, send1, recv1, send2, recv2, send3, recv3,
):
    z, b, c = lax.axis_index("sensor"), lax.axis_index("band"), lax.axis_index("win")
    groups = band_n * win_n
    g = b * win_n + c
    me = z * groups + g
    rows, samples = rows_in.shape
    part = samples // groups
    shard = alive.shape[0]
    half = LANES // 2
    local_items = item_count // groups
    ends = [sum(CHUNKS[: turn + 1]) * shard for turn in range(len(CHUNKS))]
    chunks = [(end - windows * shard, windows * shard) for end, windows in zip(ends, CHUNKS)]

    offsets = [
        (dz, db, dc) for dz in range(sensor_n) for db in range(band_n) for dc in range(win_n)
    ]

    z_high, z_low = lax.div(z, 2), lax.rem(z, 2)

    def peer(dz, db, dc):
        return (
            2 * lax.rem(z_high + dz // 2, 2) + lax.rem(z_low + dz % 2, 2),
            lax.rem(b + db, band_n),
            lax.rem(c + dc, win_n),
        )

    def ident(place):
        return {"sensor": place[0], "band": place[1], "win": place[2]}

    alive_copy = pltpu.make_async_copy(alive_hbm, alive, table_sem.at[2])
    alive_copy.start()
    basis_copy = pltpu.make_async_copy(basis_hbm, basis, table_sem.at[0])
    lag_copy = pltpu.make_async_copy(lag_hbm, lag, table_sem.at[1])

    def mine_of(group, start, count):
        return records.at[pl.ds(pl.multiple_of(group * rows + start, 16), count)]

    def columns_of(group, start, count):
        columns = pl.ds(pl.multiple_of(group * part, LANES), part)
        return rows_in.at[start : start + count, columns]

    own_copy = pltpu.make_async_copy(mine_of(g, 0, rows), columns_of(g, 0, rows), own_sem.at[0])
    own_copy.start()

    mate = ident(peer(0, 0, 1))
    first, second = c == 0, c == 1
    barrier = pltpu.get_barrier_semaphore()
    for off in offsets[1:]:
        place = peer(*off)

        @pl.when(place[2] == (0 if off[0] == 0 else 1))
        def _(place=place):
            pl.semaphore_signal(barrier, inc=1, device_id=ident(place), device_id_type=MESH)

    basis_copy.start()

    @pl.when(first)
    def _():
        pl.semaphore_wait(barrier, groups - 1)
        pl.semaphore_signal(near_sem, inc=1, device_id=mate, device_id_type=MESH)

    @pl.when(second)
    def _():
        pl.semaphore_wait(near_sem, 1)

    copies1 = {}
    for turn, (start, count) in enumerate(chunks):
        for db in reversed(range(band_n)):
            for dc in range(win_n):
                if (db, dc) == (0, 0):
                    continue
                slot = turn * groups + db * win_n + dc
                place = peer(0, db, dc)
                copy = pltpu.make_async_remote_copy(
                    src_ref=mine_of(place[1] * win_n + place[2], start, count),
                    dst_ref=columns_of(g, start, count),
                    send_sem=send1.at[slot],
                    recv_sem=recv1.at[slot],
                    device_id=ident(place),
                    device_id_type=MESH,
                )
                copy.start()
                copies1[turn, db, dc] = copy
    lag_copy.start()

    alive_copy.wait()
    row_item = lax.broadcasted_iota(jnp.int32, (rows, item_count), 0) // shard
    item = lax.broadcasted_iota(jnp.int32, (rows, item_count), 1)
    pick = jnp.where(row_item + g * local_items == item, 1.0, 0.0)
    spread_alive = lax.dot_general(
        pick.astype(jnp.bfloat16),
        alive[...].astype(jnp.float32).astype(jnp.bfloat16),
        (((1,), (1,)), ((), ())),
        preferred_element_type=jnp.float32,
    )
    row_sensor = lax.rem(lax.broadcasted_iota(jnp.int32, (rows, shard), 0), shard)
    column = lax.broadcasted_iota(jnp.int32, (rows, shard), 1)
    usable = jnp.sum(
        jnp.where(row_sensor == column, spread_alive, 0.0), axis=1, keepdims=True
    )

    own_copy.wait()
    basis_copy.wait()

    @pl.when(second)
    def _():
        pl.semaphore_wait(barrier, (sensor_n - 1) * groups)
        pl.semaphore_signal(far_sem, inc=1, device_id=mate, device_id_type=MESH)

    @pl.when(first)
    def _():
        pl.semaphore_wait(far_sem, 1)

    copies2 = {}
    order = [(dz, db) for near in ((2, 3), (1, 0)) for db in (1, 0) for dz in near]
    for turn, (start, count) in enumerate(chunks):
        lines = slice(start, start + count)
        for (at, _, _), copy in copies1.items():
            if at == turn:
                copy.wait_recv()
        for step, (dz, db) in enumerate(order):
            place_z, place_b, _ = peer(dz, db, 0)
            spectra = jnp.dot(
                rows_in[lines, :],
                basis[place_z * band_n + place_b],
                preferred_element_type=jnp.float32,
            )
            for core in range(win_n):
                piece = spectra[:, core * LANES : (core + 1) * LANES]
                square = piece * piece
                power = square + pltpu.roll(square, half, 1)
                white = piece * (lax.rsqrt(power + WHITEN_FLOOR) * usable[lines])
                outgoing[step, core, lines] = white.astype(jnp.bfloat16)
            for dc in range(win_n):
                place = peer(dz, db, dc)
                if (dz, db, dc) == (0, 0, 0):
                    spread[me, lines, :] = outgoing[step, c, lines]
                    continue
                slot = ((turn * sensor_n + dz) * band_n + db) * win_n + dc
                copy = pltpu.make_async_remote_copy(
                    src_ref=outgoing.at[step, place[2], lines],
                    dst_ref=spread.at[me, lines],
                    send_sem=send2.at[slot],
                    recv_sem=recv2.at[slot],
                    device_id=ident(place),
                    device_id_type=MESH,
                )
                copy.start()
                copies2[turn, dz, db, dc] = copy

    def send_home(home_z, home_g):
        to = home_z * groups + home_g
        block = stacked[to].astype(jnp.bfloat16)
        sending[to] = block

        @pl.when(me == to)
        def _():
            homed[me] = sending[to]

        @pl.when(me != to)
        def _():
            pltpu.make_async_remote_copy(
                src_ref=sending.at[to],
                dst_ref=homed.at[me],
                send_sem=send3.at[to],
                recv_sem=recv3.at[me],
                device_id=ident((home_z, home_g // win_n, home_g % win_n)),
                device_id_type=MESH,
            ).start()

    lane = lax.broadcasted_iota(jnp.int32, (shard, LANES), 1)
    window_scale = 1.0 / math.sqrt(item_count)
    near = [(db, dc) for db in (1, 0) for dc in range(win_n)]
    waves = [
        (turn, near[at : at + groups // splits])
        for turn, splits in enumerate(SPLITS)
        for at in range(0, groups, groups // splits)
    ]
    for stage, (turn, sources) in enumerate(waves):
        start, count = chunks[turn]
        lines = slice(start, start + count)
        step_items = count // shard
        for db, dc in sources:
            for dz in range(sensor_n):
                if (dz, db, dc) != (0, 0, 0):
                    copies2[turn, dz, db, dc].wait_recv()
        for k, (db, dc) in enumerate(sources):
            _, source_b, source_c = peer(0, db, dc)
            source_g = source_b * win_n + source_c
            items = slice(k * step_items, (k + 1) * step_items)
            for source_z in range(sensor_n):
                block = spread[source_z * groups + source_g, lines, :].astype(jnp.float32)
                wide[source_z, items] = block.reshape(step_items, shard, LANES)
                turned[source_z, items] = pltpu.roll(block, half, 1).reshape(
                    step_items, shard, LANES
                )

        for first_z in range(sensor_n):
            seconds = list(range(first_z, sensor_n))
            batch = 4 if len(seconds) > 2 else 8
            for begin in range(0, shard, batch):
                places = [
                    (second_z, part, begin + k)
                    for second_z in seconds
                    for k in range(batch)
                    for part in range(2)
                ]

                def add(w, sums, first_z=first_z, begin=begin, batch=batch, places=places):
                    left = [
                        jnp.broadcast_to(wide[first_z, w, s : s + 1, :], (shard, LANES))
                        for s in range(begin, begin + batch)
                    ]
                    right = {
                        (z2, part): (turned if part else wide)[z2, w]
                        for z2 in range(first_z, sensor_n)
                        for part in range(2)
                    }
                    return tuple(
                        total + left[s - begin] * right[z2, part]
                        for total, (z2, part, s) in zip(sums, places, strict=True)
                    )

                if stage == 0:
                    first_sums = (jnp.zeros((shard, LANES), jnp.float32),) * len(places)
                else:
                    first_sums = tuple(
                        totals[first_z * sensor_n + z2, part, s] for z2, part, s in places
                    )
                sums = lax.fori_loop(
                    0, len(sources) * step_items, add, first_sums, unroll=UNROLL
                )
                if stage < len(waves) - 1:
                    for total, (z2, part, s) in zip(sums, places, strict=True):
                        totals[first_z * sensor_n + z2, part, s] = total
                    continue
                found = dict(zip(places, sums, strict=True))
                for z2 in seconds:
                    for s in range(begin, begin + batch):
                        same, cross = found[z2, 0, s], found[z2, 1, s]
                        real = (same + pltpu.roll(same, half, 1)) * window_scale
                        imag = (cross - pltpu.roll(cross, half, 1)) * window_scale
                        stacked[first_z * groups + z2, s * shard : (s + 1) * shard, :] = jnp.where(
                            lane < half, real, imag
                        )
                        if z2 != first_z:
                            stacked[z2 * groups + first_z, pl.ds(s, shard, stride=shard), :] = (
                                jnp.where(lane < half, real, -imag)
                            )
            if stage == len(waves) - 1:
                for home_z, home_g in [(first_z, z2) for z2 in seconds] + [
                    (z2, first_z) for z2 in seconds[1:]
                ]:
                    send_home(home_z, home_g)
    lag_copy.wait()
    lagged = None
    side = sensor_n * groups // 2
    for near in ((0, 1), (2, 3)):
        for dz, db, dc in offsets:
            if dz in near and (dz, db, dc) != (0, 0, 0):
                place = peer(dz, db, dc)
                source = place[0] * groups + place[1] * win_n + place[2]
                pltpu.make_async_remote_copy(
                    src_ref=sending.at[source],
                    dst_ref=homed.at[source],
                    send_sem=send3.at[source],
                    recv_sem=recv3.at[source],
                    device_id=ident(place),
                    device_id_type=MESH,
                ).wait_recv()
        first_source = peer(near[0], 0, 0)[0] // 2 * side
        block = jnp.concatenate([homed[first_source + at] for at in range(side)], axis=1)
        depth = side * LANES
        term = jnp.dot(
            block,
            lag[pl.ds(pl.multiple_of(first_source * LANES, depth), depth)],
            preferred_element_type=jnp.float32,
        )
        lagged = term if lagged is None else lagged + term
    out[...] = lagged[:, : out.shape[1]]
    for copy in [*copies1.values(), *copies2.values()]:
        copy.wait_send()
    for off in offsets[1:]:
        place = peer(*off)
        to = place[0] * groups + place[1] * win_n + place[2]
        pltpu.make_async_remote_copy(
            src_ref=sending.at[to],
            dst_ref=homed.at[me],
            send_sem=send3.at[to],
            recv_sem=recv3.at[to],
            device_id=ident(place),
            device_id_type=MESH,
        ).wait_send()


def fused(sizes, records, alive):
    sensor_n, band_n, win_n = sizes
    groups = band_n * win_n
    peers = sensor_n * groups
    item_count, shard, part = records.shape
    samples = part * groups
    bin_count = samples // 2
    half = LANES // 2
    rows = item_count // groups * shard
    lag_count = 2 * MAXLAG + 1
    stage_items = max(groups // cut * windows for windows, cut in zip(CHUNKS, SPLITS))
    lag_room = -(-lag_count // LANES) * LANES
    table = spectrum_table(samples, bin_count).reshape(samples, 2, peers, half)
    table = table.transpose(0, 2, 1, 3).reshape(samples, peers // win_n, win_n * LANES)
    basis = np.ascontiguousarray(table.transpose(1, 0, 2))
    table = lag_table(samples, bin_count, MAXLAG).reshape(2, peers, half, lag_count)
    table = table.transpose(1, 0, 2, 3).reshape(2 * bin_count, lag_count)
    lag = np.zeros((2 * bin_count, lag_room), ml_dtypes.bfloat16)
    lag[:, :lag_count] = table
    vmem = pl.BlockSpec(memory_space=pltpu.VMEM)
    far = pl.BlockSpec(memory_space=pltpu.HBM)
    dma = pltpu.SemaphoreType.DMA
    result = pl.pallas_call(
        functools.partial(kernel, sensor_n, band_n, win_n, item_count),
        out_shape=pltpu.VMEM((shard * shard, lag_count), jnp.float32),
        in_specs=[far, far, far, far],
        out_specs=vmem,
        scratch_shapes=[
            pltpu.VMEM((shard, item_count), jnp.int32),
            pltpu.VMEM(basis.shape, jnp.bfloat16),
            pltpu.VMEM(lag.shape, jnp.bfloat16),
            pltpu.VMEM((rows, samples), jnp.bfloat16),
            pltpu.VMEM((peers // win_n, win_n, rows, LANES), jnp.bfloat16),
            pltpu.VMEM((peers, rows, LANES), jnp.bfloat16),
            pltpu.VMEM((sensor_n, stage_items, shard, LANES), jnp.float32),
            pltpu.VMEM((sensor_n, stage_items, shard, LANES), jnp.float32),
            pltpu.VMEM((peers, 2, shard, shard, LANES), jnp.float32),
            pltpu.VMEM((peers, shard * shard, LANES), jnp.float32),
            pltpu.VMEM((peers, shard * shard, LANES), jnp.bfloat16),
            pltpu.VMEM((peers, shard * shard, LANES), jnp.bfloat16),
            dma((3,)),
            dma((2,)),
            pltpu.SemaphoreType.REGULAR,
            pltpu.SemaphoreType.REGULAR,
            dma((len(CHUNKS) * groups,)),
            dma((len(CHUNKS) * groups,)),
            dma((len(CHUNKS) * peers,)),
            dma((len(CHUNKS) * peers,)),
            dma((peers,)),
            dma((peers,)),
        ],
        compiler_params=pltpu.CompilerParams(
            collective_id=0, has_side_effects=True, vmem_limit_bytes=56 << 20
        ),
    )(
        records.reshape(item_count * shard, part),
        alive.T,
        jnp.asarray(basis),
        jnp.asarray(lag),
    )
    return result.reshape(shard, shard, lag_count)


def cross_block(local_spec, incoming, window_scale):
    products = jnp.einsum(
        "wicf,nwjdf->injcdf", local_spec, incoming, preferred_element_type=jnp.float32
    )
    real_part = products[:, :, :, 0, 0] + products[:, :, :, 1, 1]
    imag_part = products[:, :, :, 1, 0] - products[:, :, :, 0, 1]
    return jnp.stack([real_part, imag_part], axis=3) * window_scale


def general(records, alive):
    groups = lax.axis_size(ROW_AXES)
    sensors_count = lax.axis_size("sensor")
    shard_sensors = records.shape[1]
    samples = records.shape[2] * groups
    bin_count = samples // 2
    bins_local = bin_count // groups
    dft_basis = jnp.asarray(spectrum_table(samples, bin_count).reshape(samples, -1))
    pieces = lax.all_to_all(records, ROW_AXES, split_axis=1, concat_axis=2, tiled=True)
    item_count = pieces.shape[0]
    sample_rows = pieces.reshape(-1, samples)
    spectra = jnp.dot(sample_rows, dft_basis, preferred_element_type=jnp.float32)
    spectra = spectra.reshape(item_count, -1, 2, bin_count)
    power_sum = spectra[:, :, 0] * spectra[:, :, 0] + spectra[:, :, 1] * spectra[:, :, 1]
    whitened = (spectra * lax.rsqrt(power_sum + WHITEN_FLOOR)[:, :, None, :]).astype(jnp.bfloat16)
    spectra = lax.all_to_all(whitened, ROW_AXES, split_axis=3, concat_axis=1, tiled=True)
    spectra = spectra * alive.astype(jnp.bfloat16)[:, :, None, None]
    window_scale = 1.0 / math.sqrt(spectra.shape[0])
    spread = lax.all_to_all(spectra, "sensor", split_axis=3, concat_axis=1, tiled=True)
    every_pair = cross_block(spread, spread[None], window_scale)[:, 0]
    paired = every_pair.astype(jnp.bfloat16)
    homed = lax.all_to_all(paired, "sensor", split_axis=0, concat_axis=3, tiled=True)
    stacked = homed.reshape(shard_sensors, sensors_count, shard_sensors, 2, bins_local)
    relaid = lax.all_to_all(stacked, ROW_AXES, split_axis=1, concat_axis=4, tiled=True)
    flattened = relaid.reshape(-1, 2 * bin_count)
    lag_basis = jnp.asarray(lag_table(samples, bin_count, MAXLAG).reshape(2 * bin_count, -1))
    lagged = jnp.dot(flattened, lag_basis, preferred_element_type=jnp.float32)
    return lagged.reshape(shard_sensors, -1, 2 * MAXLAG + 1)


def body(sizes, records, alive):
    sensor_n, band_n, win_n = sizes
    groups = band_n * win_n
    item_count, shard, part = records.shape
    fits = (
        part * groups == sensor_n * groups * LANES
        and (sensor_n, band_n, win_n) == (4, 2, 2)
        and shard == 8
        and item_count == groups * sum(CHUNKS)
        and part % LANES == 0
    )
    if fits:
        return fused(sizes, records, alive)
    return general(records, alive)


def solution(mesh):
    sizes = tuple(mesh.shape[name] for name in ("sensor", "band", "win"))
    return jax.shard_map(
        functools.partial(body, sizes),
        mesh=mesh,
        in_specs=(P("days", "sensor", ROW_AXES), P("days", "sensor")),
        out_specs=P(("days", "sensor"), ROW_AXES, None),
        check_vma=False,
    )
```

```python
import functools
import math

import jax
import jax.numpy as jnp
import ml_dtypes
import numpy as np
from jax import lax
from jax.experimental import pallas as pl
from jax.experimental.pallas import tpu as pltpu
from jax.sharding import PartitionSpec as P

MAXLAG = 300
WHITEN_FLOOR = 0.5
LANES = 128
UNROLL = 2
CHUNKS = (6, 10, 8)
SPLITS = (2, 2, 2)
ROW_AXES = ("band", "win")
MESH = pl.DeviceIdType.MESH


def spectrum_table(samples, bin_count):
    time_index = np.arange(samples, dtype=np.int64)[:, None]
    freq_index = np.arange(bin_count, dtype=np.int64)[None, :]
    phase_angle = (time_index * freq_index % samples).astype(np.float32) * np.float32(
        2.0 * math.pi / samples
    )
    phase_angle = phase_angle.astype(np.float64)
    table = np.stack([np.cos(phase_angle), -np.sin(phase_angle)], axis=1)
    table = table.astype(np.float32) / np.float32(math.sqrt(samples))
    return table.astype(ml_dtypes.bfloat16)


def lag_table(samples, bin_count, maxlag):
    lag_count = 2 * maxlag + 1
    freq_index = np.arange(bin_count, dtype=np.int64)[:, None]
    shifts = np.arange(lag_count, dtype=np.int64)[None, :] - maxlag
    phase_angle = (freq_index * shifts % samples).astype(np.float32) * np.float32(
        2.0 * math.pi / samples
    )
    phase_angle = phase_angle.astype(np.float64)
    weight = np.where(freq_index == 0, 1.0, 2.0).astype(np.float32) / np.float32(
        2.0 * math.sqrt(bin_count)
    )
    table = np.stack([np.cos(phase_angle), -np.sin(phase_angle)], axis=0)
    table = weight[None] * table.astype(np.float32)
    return table.astype(ml_dtypes.bfloat16)


def kernel(
    sensor_n, band_n, win_n, item_count,
    records, alive_hbm, basis_hbm, lag_hbm, out,
    alive, basis, lag, rows_in, outgoing, spread, wide, turned, totals, stacked, sending, homed,
    table_sem, own_sem, near_sem, far_sem, send1, recv1, send2, recv2, send3, recv3,
):
    z, b, c = lax.axis_index("sensor"), lax.axis_index("band"), lax.axis_index("win")
    groups = band_n * win_n
    g = b * win_n + c
    me = z * groups + g
    rows, samples = rows_in.shape
    part = samples // groups
    shard = alive.shape[0]
    half = LANES // 2
    local_items = item_count // groups
    ends = [sum(CHUNKS[: turn + 1]) * shard for turn in range(len(CHUNKS))]
    chunks = [(end - windows * shard, windows * shard) for end, windows in zip(ends, CHUNKS)]

    offsets = [
        (dz, db, dc) for dz in range(sensor_n) for db in range(band_n) for dc in range(win_n)
    ]

    z_high, z_low = lax.div(z, 2), lax.rem(z, 2)

    def peer(dz, db, dc):
        return (
            2 * lax.rem(z_high + dz // 2, 2) + lax.rem(z_low + dz % 2, 2),
            lax.rem(b + db, band_n),
            lax.rem(c + dc, win_n),
        )

    def ident(place):
        return {"sensor": place[0], "band": place[1], "win": place[2]}

    alive_copy = pltpu.make_async_copy(alive_hbm, alive, table_sem.at[2])
    alive_copy.start()
    basis_copy = pltpu.make_async_copy(basis_hbm, basis, table_sem.at[0])
    lag_copy = pltpu.make_async_copy(lag_hbm, lag, table_sem.at[1])

    def mine_of(group, start, count):
        return records.at[pl.ds(pl.multiple_of(group * rows + start, 16), count)]

    def columns_of(group, start, count):
        columns = pl.ds(pl.multiple_of(group * part, LANES), part)
        return rows_in.at[start : start + count, columns]

    own_copy = pltpu.make_async_copy(mine_of(g, 0, rows), columns_of(g, 0, rows), own_sem.at[0])
    own_copy.start()

    mate = ident(peer(0, 0, 1))
    first, second = c == 0, c == 1
    barrier = pltpu.get_barrier_semaphore()
    for off in offsets[1:]:
        place = peer(*off)

        @pl.when(place[2] == (0 if off[0] == 0 else 1))
        def _(place=place):
            pl.semaphore_signal(barrier, inc=1, device_id=ident(place), device_id_type=MESH)

    basis_copy.start()

    @pl.when(first)
    def _():
        pl.semaphore_wait(barrier, groups - 1)
        pl.semaphore_signal(near_sem, inc=1, device_id=mate, device_id_type=MESH)

    @pl.when(second)
    def _():
        pl.semaphore_wait(near_sem, 1)

    copies1 = {}
    for turn, (start, count) in enumerate(chunks):
        for db in reversed(range(band_n)):
            for dc in range(win_n):
                if (db, dc) == (0, 0):
                    continue
                slot = turn * groups + db * win_n + dc
                place = peer(0, db, dc)
                copy = pltpu.make_async_remote_copy(
                    src_ref=mine_of(place[1] * win_n + place[2], start, count),
                    dst_ref=columns_of(g, start, count),
                    send_sem=send1.at[slot],
                    recv_sem=recv1.at[slot],
                    device_id=ident(place),
                    device_id_type=MESH,
                )
                copy.start()
                copies1[turn, db, dc] = copy
    lag_copy.start()

    alive_copy.wait()
    row_item = lax.broadcasted_iota(jnp.int32, (rows, item_count), 0) // shard
    item = lax.broadcasted_iota(jnp.int32, (rows, item_count), 1)
    pick = jnp.where(row_item + g * local_items == item, 1.0, 0.0)
    spread_alive = lax.dot_general(
        pick.astype(jnp.bfloat16),
        alive[...].astype(jnp.float32).astype(jnp.bfloat16),
        (((1,), (1,)), ((), ())),
        preferred_element_type=jnp.float32,
    )
    row_sensor = lax.rem(lax.broadcasted_iota(jnp.int32, (rows, shard), 0), shard)
    column = lax.broadcasted_iota(jnp.int32, (rows, shard), 1)
    usable = jnp.sum(
        jnp.where(row_sensor == column, spread_alive, 0.0), axis=1, keepdims=True
    )

    own_copy.wait()
    basis_copy.wait()

    @pl.when(second)
    def _():
        pl.semaphore_wait(barrier, (sensor_n - 1) * groups)
        pl.semaphore_signal(far_sem, inc=1, device_id=mate, device_id_type=MESH)

    @pl.when(first)
    def _():
        pl.semaphore_wait(far_sem, 1)

    copies2 = {}
    order = [(dz, db) for near in ((2, 3), (1, 0)) for db in (1, 0) for dz in near]
    for turn, (start, count) in enumerate(chunks):
        lines = slice(start, start + count)
        for (at, _, _), copy in copies1.items():
            if at == turn:
                copy.wait_recv()
        for step, (dz, db) in enumerate(order):
            place_z, place_b, _ = peer(dz, db, 0)
            spectra = jnp.dot(
                rows_in[lines, :],
                basis[place_z * band_n + place_b],
                preferred_element_type=jnp.float32,
            )
            for core in range(win_n):
                piece = spectra[:, core * LANES : (core + 1) * LANES]
                square = piece * piece
                power = square + pltpu.roll(square, half, 1)
                white = piece * (lax.rsqrt(power + WHITEN_FLOOR) * usable[lines])
                outgoing[step, core, lines] = white.astype(jnp.bfloat16)
            for dc in range(win_n):
                place = peer(dz, db, dc)
                if (dz, db, dc) == (0, 0, 0):
                    spread[me, lines, :] = outgoing[step, c, lines]
                    continue
                slot = ((turn * sensor_n + dz) * band_n + db) * win_n + dc
                copy = pltpu.make_async_remote_copy(
                    src_ref=outgoing.at[step, place[2], lines],
                    dst_ref=spread.at[me, lines],
                    send_sem=send2.at[slot],
                    recv_sem=recv2.at[slot],
                    device_id=ident(place),
                    device_id_type=MESH,
                )
                copy.start()
                copies2[turn, dz, db, dc] = copy

    def send_home(home_z, home_g):
        to = home_z * groups + home_g
        block = stacked[to].astype(jnp.bfloat16)
        sending[to] = block

        @pl.when(me == to)
        def _():
            homed[me] = sending[to]

        @pl.when(me != to)
        def _():
            pltpu.make_async_remote_copy(
                src_ref=sending.at[to],
                dst_ref=homed.at[me],
                send_sem=send3.at[to],
                recv_sem=recv3.at[me],
                device_id=ident((home_z, home_g // win_n, home_g % win_n)),
                device_id_type=MESH,
            ).start()

    lane = lax.broadcasted_iota(jnp.int32, (shard, LANES), 1)
    window_scale = 1.0 / math.sqrt(item_count)
    near = [(db, dc) for db in (1, 0) for dc in range(win_n)]
    waves = [
        (turn, near[at : at + groups // splits])
        for turn, splits in enumerate(SPLITS)
        for at in range(0, groups, groups // splits)
    ]
    for stage, (turn, sources) in enumerate(waves):
        start, count = chunks[turn]
        lines = slice(start, start + count)
        step_items = count // shard
        for db, dc in sources:
            for dz in range(sensor_n):
                if (dz, db, dc) != (0, 0, 0):
                    copies2[turn, dz, db, dc].wait_recv()
        for k, (db, dc) in enumerate(sources):
            _, source_b, source_c = peer(0, db, dc)
            source_g = source_b * win_n + source_c
            items = slice(k * step_items, (k + 1) * step_items)
            for source_z in range(sensor_n):
                block = spread[source_z * groups + source_g, lines, :].astype(jnp.float32)
                wide[source_z, items] = block.reshape(step_items, shard, LANES)
                turned[source_z, items] = pltpu.roll(block, half, 1).reshape(
                    step_items, shard, LANES
                )

        for first_z in range(sensor_n):
            seconds = list(range(first_z, sensor_n))
            batch = 4 if len(seconds) > 2 else 8
            for begin in range(0, shard, batch):
                places = [
                    (second_z, part, begin + k)
                    for second_z in seconds
                    for k in range(batch)
                    for part in range(2)
                ]

                def add(w, sums, first_z=first_z, begin=begin, batch=batch, places=places):
                    left = [
                        jnp.broadcast_to(wide[first_z, w, s : s + 1, :], (shard, LANES))
                        for s in range(begin, begin + batch)
                    ]
                    right = {
                        (z2, part): (turned if part else wide)[z2, w]
                        for z2 in range(first_z, sensor_n)
                        for part in range(2)
                    }
                    return tuple(
                        total + left[s - begin] * right[z2, part]
                        for total, (z2, part, s) in zip(sums, places, strict=True)
                    )

                if stage == 0:
                    first_sums = (jnp.zeros((shard, LANES), jnp.float32),) * len(places)
                else:
                    first_sums = tuple(
                        totals[first_z * sensor_n + z2, part, s] for z2, part, s in places
                    )
                sums = lax.fori_loop(
                    0, len(sources) * step_items, add, first_sums, unroll=UNROLL
                )
                if stage < len(waves) - 1:
                    for total, (z2, part, s) in zip(sums, places, strict=True):
                        totals[first_z * sensor_n + z2, part, s] = total
                    continue
                found = dict(zip(places, sums, strict=True))
                for z2 in seconds:
                    for s in range(begin, begin + batch):
                        same, cross = found[z2, 0, s], found[z2, 1, s]
                        real = (same + pltpu.roll(same, half, 1)) * window_scale
                        imag = (cross - pltpu.roll(cross, half, 1)) * window_scale
                        stacked[first_z * groups + z2, s * shard : (s + 1) * shard, :] = jnp.where(
                            lane < half, real, imag
                        )
                        if z2 != first_z:
                            stacked[z2 * groups + first_z, pl.ds(s, shard, stride=shard), :] = (
                                jnp.where(lane < half, real, -imag)
                            )
            if stage == len(waves) - 1:
                for home_z, home_g in [(first_z, z2) for z2 in seconds] + [
                    (z2, first_z) for z2 in seconds[1:]
                ]:
                    send_home(home_z, home_g)
    lag_copy.wait()
    lagged = None
    for near in range(sensor_n):
        for dz, db, dc in offsets:
            if dz == near and (dz, db, dc) != (0, 0, 0):
                place = peer(dz, db, dc)
                source = place[0] * groups + place[1] * win_n + place[2]
                pltpu.make_async_remote_copy(
                    src_ref=sending.at[source],
                    dst_ref=homed.at[source],
                    send_sem=send3.at[source],
                    recv_sem=recv3.at[source],
                    device_id=ident(place),
                    device_id_type=MESH,
                ).wait_recv()
        first_source = peer(near, 0, 0)[0] * groups
        block = jnp.concatenate([homed[first_source + at] for at in range(groups)], axis=1)
        depth = groups * LANES
        term = jnp.dot(
            block,
            lag[pl.ds(pl.multiple_of(first_source * LANES, depth), depth)],
            preferred_element_type=jnp.float32,
        )
        lagged = term if lagged is None else lagged + term
    out[...] = lagged[:, : out.shape[1]]
    for copy in [*copies1.values(), *copies2.values()]:
        copy.wait_send()
    for off in offsets[1:]:
        place = peer(*off)
        to = place[0] * groups + place[1] * win_n + place[2]
        pltpu.make_async_remote_copy(
            src_ref=sending.at[to],
            dst_ref=homed.at[me],
            send_sem=send3.at[to],
            recv_sem=recv3.at[to],
            device_id=ident(place),
            device_id_type=MESH,
        ).wait_send()


def fused(sizes, records, alive):
    sensor_n, band_n, win_n = sizes
    groups = band_n * win_n
    peers = sensor_n * groups
    item_count, shard, part = records.shape
    samples = part * groups
    bin_count = samples // 2
    half = LANES // 2
    rows = item_count // groups * shard
    lag_count = 2 * MAXLAG + 1
    stage_items = max(groups // cut * windows for windows, cut in zip(CHUNKS, SPLITS))
    lag_room = -(-lag_count // LANES) * LANES
    table = spectrum_table(samples, bin_count).reshape(samples, 2, peers, half)
    table = table.transpose(0, 2, 1, 3).reshape(samples, peers // win_n, win_n * LANES)
    basis = np.ascontiguousarray(table.transpose(1, 0, 2))
    table = lag_table(samples, bin_count, MAXLAG).reshape(2, peers, half, lag_count)
    table = table.transpose(1, 0, 2, 3).reshape(2 * bin_count, lag_count)
    lag = np.zeros((2 * bin_count, lag_room), ml_dtypes.bfloat16)
    lag[:, :lag_count] = table
    vmem = pl.BlockSpec(memory_space=pltpu.VMEM)
    far = pl.BlockSpec(memory_space=pltpu.HBM)
    dma = pltpu.SemaphoreType.DMA
    result = pl.pallas_call(
        functools.partial(kernel, sensor_n, band_n, win_n, item_count),
        out_shape=pltpu.VMEM((shard * shard, lag_count), jnp.float32),
        in_specs=[far, far, far, far],
        out_specs=vmem,
        scratch_shapes=[
            pltpu.VMEM((shard, item_count), jnp.int32),
            pltpu.VMEM(basis.shape, jnp.bfloat16),
            pltpu.VMEM(lag.shape, jnp.bfloat16),
            pltpu.VMEM((rows, samples), jnp.bfloat16),
            pltpu.VMEM((peers // win_n, win_n, rows, LANES), jnp.bfloat16),
            pltpu.VMEM((peers, rows, LANES), jnp.bfloat16),
            pltpu.VMEM((sensor_n, stage_items, shard, LANES), jnp.float32),
            pltpu.VMEM((sensor_n, stage_items, shard, LANES), jnp.float32),
            pltpu.VMEM((peers, 2, shard, shard, LANES), jnp.float32),
            pltpu.VMEM((peers, shard * shard, LANES), jnp.float32),
            pltpu.VMEM((peers, shard * shard, LANES), jnp.bfloat16),
            pltpu.VMEM((peers, shard * shard, LANES), jnp.bfloat16),
            dma((3,)),
            dma((2,)),
            pltpu.SemaphoreType.REGULAR,
            pltpu.SemaphoreType.REGULAR,
            dma((len(CHUNKS) * groups,)),
            dma((len(CHUNKS) * groups,)),
            dma((len(CHUNKS) * peers,)),
            dma((len(CHUNKS) * peers,)),
            dma((peers,)),
            dma((peers,)),
        ],
        compiler_params=pltpu.CompilerParams(
            collective_id=0, has_side_effects=True, vmem_limit_bytes=56 << 20
        ),
    )(
        records.reshape(item_count * shard, part),
        alive.T,
        jnp.asarray(basis),
        jnp.asarray(lag),
    )
    return result.reshape(shard, shard, lag_count)


def cross_block(local_spec, incoming, window_scale):
    products = jnp.einsum(
        "wicf,nwjdf->injcdf", local_spec, incoming, preferred_element_type=jnp.float32
    )
    real_part = products[:, :, :, 0, 0] + products[:, :, :, 1, 1]
    imag_part = products[:, :, :, 1, 0] - products[:, :, :, 0, 1]
    return jnp.stack([real_part, imag_part], axis=3) * window_scale


def general(records, alive):
    groups = lax.axis_size(ROW_AXES)
    sensors_count = lax.axis_size("sensor")
    shard_sensors = records.shape[1]
    samples = records.shape[2] * groups
    bin_count = samples // 2
    bins_local = bin_count // groups
    dft_basis = jnp.asarray(spectrum_table(samples, bin_count).reshape(samples, -1))
    pieces = lax.all_to_all(records, ROW_AXES, split_axis=1, concat_axis=2, tiled=True)
    item_count = pieces.shape[0]
    sample_rows = pieces.reshape(-1, samples)
    spectra = jnp.dot(sample_rows, dft_basis, preferred_element_type=jnp.float32)
    spectra = spectra.reshape(item_count, -1, 2, bin_count)
    power_sum = spectra[:, :, 0] * spectra[:, :, 0] + spectra[:, :, 1] * spectra[:, :, 1]
    whitened = (spectra * lax.rsqrt(power_sum + WHITEN_FLOOR)[:, :, None, :]).astype(jnp.bfloat16)
    spectra = lax.all_to_all(whitened, ROW_AXES, split_axis=3, concat_axis=1, tiled=True)
    spectra = spectra * alive.astype(jnp.bfloat16)[:, :, None, None]
    window_scale = 1.0 / math.sqrt(spectra.shape[0])
    spread = lax.all_to_all(spectra, "sensor", split_axis=3, concat_axis=1, tiled=True)
    every_pair = cross_block(spread, spread[None], window_scale)[:, 0]
    paired = every_pair.astype(jnp.bfloat16)
    homed = lax.all_to_all(paired, "sensor", split_axis=0, concat_axis=3, tiled=True)
    stacked = homed.reshape(shard_sensors, sensors_count, shard_sensors, 2, bins_local)
    relaid = lax.all_to_all(stacked, ROW_AXES, split_axis=1, concat_axis=4, tiled=True)
    flattened = relaid.reshape(-1, 2 * bin_count)
    lag_basis = jnp.asarray(lag_table(samples, bin_count, MAXLAG).reshape(2 * bin_count, -1))
    lagged = jnp.dot(flattened, lag_basis, preferred_element_type=jnp.float32)
    return lagged.reshape(shard_sensors, -1, 2 * MAXLAG + 1)


def body(sizes, records, alive):
    sensor_n, band_n, win_n = sizes
    groups = band_n * win_n
    item_count, shard, part = records.shape
    fits = (
        part * groups == sensor_n * groups * LANES
        and (sensor_n, band_n, win_n) == (4, 2, 2)
        and shard == 8
        and item_count == groups * sum(CHUNKS)
        and part % LANES == 0
    )
    if fits:
        return fused(sizes, records, alive)
    return general(records, alive)


def solution(mesh):
    sizes = tuple(mesh.shape[name] for name in ("sensor", "band", "win"))
    return jax.shard_map(
        functools.partial(body, sizes),
        mesh=mesh,
        in_specs=(P("days", "sensor", ROW_AXES), P("days", "sensor")),
        out_specs=P(("days", "sensor"), ROW_AXES, None),
        check_vma=False,
    )
```

```python
import functools
import math

import jax
import jax.numpy as jnp
import ml_dtypes
import numpy as np
from jax import lax
from jax.experimental import pallas as pl
from jax.experimental.pallas import tpu as pltpu
from jax.sharding import PartitionSpec as P

MAXLAG = 300
WHITEN_FLOOR = 0.5
LANES = 128
UNROLL = 2
CHUNKS = (6, 8, 10)
SPLITS = (2, 2, 2)
ROW_AXES = ("band", "win")
MESH = pl.DeviceIdType.MESH


def spectrum_table(samples, bin_count):
    time_index = np.arange(samples, dtype=np.int64)[:, None]
    freq_index = np.arange(bin_count, dtype=np.int64)[None, :]
    phase_angle = (time_index * freq_index % samples).astype(np.float32) * np.float32(
        2.0 * math.pi / samples
    )
    phase_angle = phase_angle.astype(np.float64)
    table = np.stack([np.cos(phase_angle), -np.sin(phase_angle)], axis=1)
    table = table.astype(np.float32) / np.float32(math.sqrt(samples))
    return table.astype(ml_dtypes.bfloat16)


def lag_table(samples, bin_count, maxlag):
    lag_count = 2 * maxlag + 1
    freq_index = np.arange(bin_count, dtype=np.int64)[:, None]
    shifts = np.arange(lag_count, dtype=np.int64)[None, :] - maxlag
    phase_angle = (freq_index * shifts % samples).astype(np.float32) * np.float32(
        2.0 * math.pi / samples
    )
    phase_angle = phase_angle.astype(np.float64)
    weight = np.where(freq_index == 0, 1.0, 2.0).astype(np.float32) / np.float32(
        2.0 * math.sqrt(bin_count)
    )
    table = np.stack([np.cos(phase_angle), -np.sin(phase_angle)], axis=0)
    table = weight[None] * table.astype(np.float32)
    return table.astype(ml_dtypes.bfloat16)


def kernel(
    sensor_n, band_n, win_n, item_count,
    records, alive_hbm, basis_hbm, lag_hbm, out,
    alive, basis, lag, rows_in, outgoing, spread, wide, turned, totals, stacked, sending, homed,
    table_sem, own_sem, near_sem, far_sem, send1, recv1, send2, recv2, send3, recv3,
):
    z, b, c = lax.axis_index("sensor"), lax.axis_index("band"), lax.axis_index("win")
    groups = band_n * win_n
    g = b * win_n + c
    me = z * groups + g
    rows, samples = rows_in.shape
    part = samples // groups
    shard = alive.shape[0]
    half = LANES // 2
    local_items = item_count // groups
    ends = [sum(CHUNKS[: turn + 1]) * shard for turn in range(len(CHUNKS))]
    chunks = [(end - windows * shard, windows * shard) for end, windows in zip(ends, CHUNKS)]

    offsets = [
        (dz, db, dc) for dz in range(sensor_n) for db in range(band_n) for dc in range(win_n)
    ]

    z_high, z_low = lax.div(z, 2), lax.rem(z, 2)

    def peer(dz, db, dc):
        return (
            2 * lax.rem(z_high + dz // 2, 2) + lax.rem(z_low + dz % 2, 2),
            lax.rem(b + db, band_n),
            lax.rem(c + dc, win_n),
        )

    def ident(place):
        return {"sensor": place[0], "band": place[1], "win": place[2]}

    alive_copy = pltpu.make_async_copy(alive_hbm, alive, table_sem.at[2])
    alive_copy.start()
    basis_copy = pltpu.make_async_copy(basis_hbm, basis, table_sem.at[0])
    lag_copy = pltpu.make_async_copy(lag_hbm, lag, table_sem.at[1])

    def mine_of(group, start, count):
        return records.at[pl.ds(pl.multiple_of(group * rows + start, 16), count)]

    def columns_of(group, start, count):
        columns = pl.ds(pl.multiple_of(group * part, LANES), part)
        return rows_in.at[start : start + count, columns]

    own_copy = pltpu.make_async_copy(mine_of(g, 0, rows), columns_of(g, 0, rows), own_sem.at[0])
    own_copy.start()

    mate = ident(peer(0, 0, 1))
    first, second = c == 0, c == 1
    barrier = pltpu.get_barrier_semaphore()
    for off in offsets[1:]:
        place = peer(*off)

        @pl.when(place[2] == (0 if off[0] == 0 else 1))
        def _(place=place):
            pl.semaphore_signal(barrier, inc=1, device_id=ident(place), device_id_type=MESH)

    basis_copy.start()

    @pl.when(first)
    def _():
        pl.semaphore_wait(barrier, groups - 1)
        pl.semaphore_signal(near_sem, inc=1, device_id=mate, device_id_type=MESH)

    @pl.when(second)
    def _():
        pl.semaphore_wait(near_sem, 1)

    copies1 = {}
    for turn, (start, count) in enumerate(chunks):
        for db in reversed(range(band_n)):
            for dc in range(win_n):
                if (db, dc) == (0, 0):
                    continue
                slot = turn * groups + db * win_n + dc
                place = peer(0, db, dc)
                copy = pltpu.make_async_remote_copy(
                    src_ref=mine_of(place[1] * win_n + place[2], start, count),
                    dst_ref=columns_of(g, start, count),
                    send_sem=send1.at[slot],
                    recv_sem=recv1.at[slot],
                    device_id=ident(place),
                    device_id_type=MESH,
                )
                copy.start()
                copies1[turn, db, dc] = copy
    lag_copy.start()

    alive_copy.wait()
    row_item = lax.broadcasted_iota(jnp.int32, (rows, item_count), 0) // shard
    item = lax.broadcasted_iota(jnp.int32, (rows, item_count), 1)
    pick = jnp.where(row_item + g * local_items == item, 1.0, 0.0)
    spread_alive = lax.dot_general(
        pick.astype(jnp.bfloat16),
        alive[...].astype(jnp.float32).astype(jnp.bfloat16),
        (((1,), (1,)), ((), ())),
        preferred_element_type=jnp.float32,
    )
    row_sensor = lax.rem(lax.broadcasted_iota(jnp.int32, (rows, shard), 0), shard)
    column = lax.broadcasted_iota(jnp.int32, (rows, shard), 1)
    usable = jnp.sum(
        jnp.where(row_sensor == column, spread_alive, 0.0), axis=1, keepdims=True
    )

    own_copy.wait()
    basis_copy.wait()

    @pl.when(second)
    def _():
        pl.semaphore_wait(barrier, (sensor_n - 1) * groups)
        pl.semaphore_signal(far_sem, inc=1, device_id=mate, device_id_type=MESH)

    @pl.when(first)
    def _():
        pl.semaphore_wait(far_sem, 1)

    copies2 = {}
    order = [(dz, db) for near in ((2, 3), (1, 0)) for db in (1, 0) for dz in near]
    for turn, (start, count) in enumerate(chunks):
        lines = slice(start, start + count)
        for (at, _, _), copy in copies1.items():
            if at == turn:
                copy.wait_recv()
        if turn == len(chunks) - 1:
            order = [(dz, db) for db in (1, 0) for dz in (2, 3, 1, 0)]
        for step, (dz, db) in enumerate(order):
            place_z, place_b, _ = peer(dz, db, 0)
            spectra = jnp.dot(
                rows_in[lines, :],
                basis[place_z * band_n + place_b],
                preferred_element_type=jnp.float32,
            )
            for core in range(win_n):
                piece = spectra[:, core * LANES : (core + 1) * LANES]
                square = piece * piece
                power = square + pltpu.roll(square, half, 1)
                white = piece * (lax.rsqrt(power + WHITEN_FLOOR) * usable[lines])
                outgoing[step, core, lines] = white.astype(jnp.bfloat16)
            for dc in range(win_n):
                place = peer(dz, db, dc)
                if (dz, db, dc) == (0, 0, 0):
                    spread[me, lines, :] = outgoing[step, c, lines]
                    continue
                slot = ((turn * sensor_n + dz) * band_n + db) * win_n + dc
                copy = pltpu.make_async_remote_copy(
                    src_ref=outgoing.at[step, place[2], lines],
                    dst_ref=spread.at[me, lines],
                    send_sem=send2.at[slot],
                    recv_sem=recv2.at[slot],
                    device_id=ident(place),
                    device_id_type=MESH,
                )
                copy.start()
                copies2[turn, dz, db, dc] = copy

    def send_home(home_z, home_g):
        to = home_z * groups + home_g
        block = stacked[to].astype(jnp.bfloat16)
        sending[to] = block

        @pl.when(me == to)
        def _():
            homed[me] = sending[to]

        @pl.when(me != to)
        def _():
            pltpu.make_async_remote_copy(
                src_ref=sending.at[to],
                dst_ref=homed.at[me],
                send_sem=send3.at[to],
                recv_sem=recv3.at[me],
                device_id=ident((home_z, home_g // win_n, home_g % win_n)),
                device_id_type=MESH,
            ).start()

    lane = lax.broadcasted_iota(jnp.int32, (shard, LANES), 1)
    window_scale = 1.0 / math.sqrt(item_count)
    near = [(db, dc) for db in (1, 0) for dc in range(win_n)]
    waves = [
        (turn, near[at : at + groups // splits])
        for turn, splits in enumerate(SPLITS)
        for at in range(0, groups, groups // splits)
    ]
    for stage, (turn, sources) in enumerate(waves):
        start, count = chunks[turn]
        lines = slice(start, start + count)
        step_items = count // shard
        for db, dc in sources:
            for dz in range(sensor_n):
                if (dz, db, dc) != (0, 0, 0):
                    copies2[turn, dz, db, dc].wait_recv()
        for k, (db, dc) in enumerate(sources):
            _, source_b, source_c = peer(0, db, dc)
            source_g = source_b * win_n + source_c
            items = slice(k * step_items, (k + 1) * step_items)
            for source_z in range(sensor_n):
                block = spread[source_z * groups + source_g, lines, :].astype(jnp.float32)
                wide[source_z, items] = block.reshape(step_items, shard, LANES)
                turned[source_z, items] = pltpu.roll(block, half, 1).reshape(
                    step_items, shard, LANES
                )

        for first_z in range(sensor_n):
            seconds = list(range(first_z, sensor_n))
            batch = 4 if len(seconds) > 2 else 8
            for begin in range(0, shard, batch):
                places = [
                    (second_z, part, begin + k)
                    for second_z in seconds
                    for k in range(batch)
                    for part in range(2)
                ]

                def add(w, sums, first_z=first_z, begin=begin, batch=batch, places=places):
                    left = [
                        jnp.broadcast_to(wide[first_z, w, s : s + 1, :], (shard, LANES))
                        for s in range(begin, begin + batch)
                    ]
                    right = {
                        (z2, part): (turned if part else wide)[z2, w]
                        for z2 in range(first_z, sensor_n)
                        for part in range(2)
                    }
                    return tuple(
                        total + left[s - begin] * right[z2, part]
                        for total, (z2, part, s) in zip(sums, places, strict=True)
                    )

                if stage == 0:
                    first_sums = (jnp.zeros((shard, LANES), jnp.float32),) * len(places)
                else:
                    first_sums = tuple(
                        totals[first_z * sensor_n + z2, part, s] for z2, part, s in places
                    )
                sums = lax.fori_loop(
                    0, len(sources) * step_items, add, first_sums, unroll=UNROLL
                )
                if stage < len(waves) - 1:
                    for total, (z2, part, s) in zip(sums, places, strict=True):
                        totals[first_z * sensor_n + z2, part, s] = total
                    continue
                found = dict(zip(places, sums, strict=True))
                for z2 in seconds:
                    for s in range(begin, begin + batch):
                        same, cross = found[z2, 0, s], found[z2, 1, s]
                        real = (same + pltpu.roll(same, half, 1)) * window_scale
                        imag = (cross - pltpu.roll(cross, half, 1)) * window_scale
                        stacked[first_z * groups + z2, s * shard : (s + 1) * shard, :] = jnp.where(
                            lane < half, real, imag
                        )
                        if z2 != first_z:
                            stacked[z2 * groups + first_z, pl.ds(s, shard, stride=shard), :] = (
                                jnp.where(lane < half, real, -imag)
                            )
            if stage == len(waves) - 1:
                for home_z, home_g in [(first_z, z2) for z2 in seconds] + [
                    (z2, first_z) for z2 in seconds[1:]
                ]:
                    send_home(home_z, home_g)
    lag_copy.wait()
    lagged = None
    for near in range(sensor_n):
        for dz, db, dc in offsets:
            if dz == near and (dz, db, dc) != (0, 0, 0):
                place = peer(dz, db, dc)
                source = place[0] * groups + place[1] * win_n + place[2]
                pltpu.make_async_remote_copy(
                    src_ref=sending.at[source],
                    dst_ref=homed.at[source],
                    send_sem=send3.at[source],
                    recv_sem=recv3.at[source],
                    device_id=ident(place),
                    device_id_type=MESH,
                ).wait_recv()
        first_source = peer(near, 0, 0)[0] * groups
        block = jnp.concatenate([homed[first_source + at] for at in range(groups)], axis=1)
        depth = groups * LANES
        term = jnp.dot(
            block,
            lag[pl.ds(pl.multiple_of(first_source * LANES, depth), depth)],
            preferred_element_type=jnp.float32,
        )
        lagged = term if lagged is None else lagged + term
    out[...] = lagged[:, : out.shape[1]]
    for copy in [*copies1.values(), *copies2.values()]:
        copy.wait_send()
    for off in offsets[1:]:
        place = peer(*off)
        to = place[0] * groups + place[1] * win_n + place[2]
        pltpu.make_async_remote_copy(
            src_ref=sending.at[to],
            dst_ref=homed.at[me],
            send_sem=send3.at[to],
            recv_sem=recv3.at[to],
            device_id=ident(place),
            device_id_type=MESH,
        ).wait_send()


def fused(sizes, records, alive):
    sensor_n, band_n, win_n = sizes
    groups = band_n * win_n
    peers = sensor_n * groups
    item_count, shard, part = records.shape
    samples = part * groups
    bin_count = samples // 2
    half = LANES // 2
    rows = item_count // groups * shard
    lag_count = 2 * MAXLAG + 1
    stage_items = max(groups // cut * windows for windows, cut in zip(CHUNKS, SPLITS))
    lag_room = -(-lag_count // LANES) * LANES
    table = spectrum_table(samples, bin_count).reshape(samples, 2, peers, half)
    table = table.transpose(0, 2, 1, 3).reshape(samples, peers // win_n, win_n * LANES)
    basis = np.ascontiguousarray(table.transpose(1, 0, 2))
    table = lag_table(samples, bin_count, MAXLAG).reshape(2, peers, half, lag_count)
    table = table.transpose(1, 0, 2, 3).reshape(2 * bin_count, lag_count)
    lag = np.zeros((2 * bin_count, lag_room), ml_dtypes.bfloat16)
    lag[:, :lag_count] = table
    vmem = pl.BlockSpec(memory_space=pltpu.VMEM)
    far = pl.BlockSpec(memory_space=pltpu.HBM)
    dma = pltpu.SemaphoreType.DMA
    result = pl.pallas_call(
        functools.partial(kernel, sensor_n, band_n, win_n, item_count),
        out_shape=pltpu.VMEM((shard * shard, lag_count), jnp.float32),
        in_specs=[far, far, far, far],
        out_specs=vmem,
        scratch_shapes=[
            pltpu.VMEM((shard, item_count), jnp.int32),
            pltpu.VMEM(basis.shape, jnp.bfloat16),
            pltpu.VMEM(lag.shape, jnp.bfloat16),
            pltpu.VMEM((rows, samples), jnp.bfloat16),
            pltpu.VMEM((peers // win_n, win_n, rows, LANES), jnp.bfloat16),
            pltpu.VMEM((peers, rows, LANES), jnp.bfloat16),
            pltpu.VMEM((sensor_n, stage_items, shard, LANES), jnp.float32),
            pltpu.VMEM((sensor_n, stage_items, shard, LANES), jnp.float32),
            pltpu.VMEM((peers, 2, shard, shard, LANES), jnp.float32),
            pltpu.VMEM((peers, shard * shard, LANES), jnp.float32),
            pltpu.VMEM((peers, shard * shard, LANES), jnp.bfloat16),
            pltpu.VMEM((peers, shard * shard, LANES), jnp.bfloat16),
            dma((3,)),
            dma((2,)),
            pltpu.SemaphoreType.REGULAR,
            pltpu.SemaphoreType.REGULAR,
            dma((len(CHUNKS) * groups,)),
            dma((len(CHUNKS) * groups,)),
            dma((len(CHUNKS) * peers,)),
            dma((len(CHUNKS) * peers,)),
            dma((peers,)),
            dma((peers,)),
        ],
        compiler_params=pltpu.CompilerParams(
            collective_id=0, has_side_effects=True, vmem_limit_bytes=56 << 20
        ),
    )(
        records.reshape(item_count * shard, part),
        alive.T,
        jnp.asarray(basis),
        jnp.asarray(lag),
    )
    return result.reshape(shard, shard, lag_count)


def cross_block(local_spec, incoming, window_scale):
    products = jnp.einsum(
        "wicf,nwjdf->injcdf", local_spec, incoming, preferred_element_type=jnp.float32
    )
    real_part = products[:, :, :, 0, 0] + products[:, :, :, 1, 1]
    imag_part = products[:, :, :, 1, 0] - products[:, :, :, 0, 1]
    return jnp.stack([real_part, imag_part], axis=3) * window_scale


def general(records, alive):
    groups = lax.axis_size(ROW_AXES)
    sensors_count = lax.axis_size("sensor")
    shard_sensors = records.shape[1]
    samples = records.shape[2] * groups
    bin_count = samples // 2
    bins_local = bin_count // groups
    dft_basis = jnp.asarray(spectrum_table(samples, bin_count).reshape(samples, -1))
    pieces = lax.all_to_all(records, ROW_AXES, split_axis=1, concat_axis=2, tiled=True)
    item_count = pieces.shape[0]
    sample_rows = pieces.reshape(-1, samples)
    spectra = jnp.dot(sample_rows, dft_basis, preferred_element_type=jnp.float32)
    spectra = spectra.reshape(item_count, -1, 2, bin_count)
    power_sum = spectra[:, :, 0] * spectra[:, :, 0] + spectra[:, :, 1] * spectra[:, :, 1]
    whitened = (spectra * lax.rsqrt(power_sum + WHITEN_FLOOR)[:, :, None, :]).astype(jnp.bfloat16)
    spectra = lax.all_to_all(whitened, ROW_AXES, split_axis=3, concat_axis=1, tiled=True)
    spectra = spectra * alive.astype(jnp.bfloat16)[:, :, None, None]
    window_scale = 1.0 / math.sqrt(spectra.shape[0])
    spread = lax.all_to_all(spectra, "sensor", split_axis=3, concat_axis=1, tiled=True)
    every_pair = cross_block(spread, spread[None], window_scale)[:, 0]
    paired = every_pair.astype(jnp.bfloat16)
    homed = lax.all_to_all(paired, "sensor", split_axis=0, concat_axis=3, tiled=True)
    stacked = homed.reshape(shard_sensors, sensors_count, shard_sensors, 2, bins_local)
    relaid = lax.all_to_all(stacked, ROW_AXES, split_axis=1, concat_axis=4, tiled=True)
    flattened = relaid.reshape(-1, 2 * bin_count)
    lag_basis = jnp.asarray(lag_table(samples, bin_count, MAXLAG).reshape(2 * bin_count, -1))
    lagged = jnp.dot(flattened, lag_basis, preferred_element_type=jnp.float32)
    return lagged.reshape(shard_sensors, -1, 2 * MAXLAG + 1)


def body(sizes, records, alive):
    sensor_n, band_n, win_n = sizes
    groups = band_n * win_n
    item_count, shard, part = records.shape
    fits = (
        part * groups == sensor_n * groups * LANES
        and (sensor_n, band_n, win_n) == (4, 2, 2)
        and shard == 8
        and item_count == groups * sum(CHUNKS)
        and part % LANES == 0
    )
    if fits:
        return fused(sizes, records, alive)
    return general(records, alive)


def solution(mesh):
    sizes = tuple(mesh.shape[name] for name in ("sensor", "band", "win"))
    return jax.shard_map(
        functools.partial(body, sizes),
        mesh=mesh,
        in_specs=(P("days", "sensor", ROW_AXES), P("days", "sensor")),
        out_specs=P(("days", "sensor"), ROW_AXES, None),
        check_vma=False,
    )
```

```python
import functools
import math

import jax
import jax.numpy as jnp
import ml_dtypes
import numpy as np
from jax import lax
from jax.experimental import pallas as pl
from jax.experimental.pallas import tpu as pltpu
from jax.sharding import PartitionSpec as P

MAXLAG = 300
WHITEN_FLOOR = 0.5
LANES = 128
UNROLL = 2
CHUNKS = (6, 8, 10)
SPLITS = (1, 1, 2)
ROW_AXES = ("band", "win")
MESH = pl.DeviceIdType.MESH


def spectrum_table(samples, bin_count):
    time_index = np.arange(samples, dtype=np.int64)[:, None]
    freq_index = np.arange(bin_count, dtype=np.int64)[None, :]
    phase_angle = (time_index * freq_index % samples).astype(np.float32) * np.float32(
        2.0 * math.pi / samples
    )
    phase_angle = phase_angle.astype(np.float64)
    table = np.stack([np.cos(phase_angle), -np.sin(phase_angle)], axis=1)
    table = table.astype(np.float32) / np.float32(math.sqrt(samples))
    return table.astype(ml_dtypes.bfloat16)


def lag_table(samples, bin_count, maxlag):
    lag_count = 2 * maxlag + 1
    freq_index = np.arange(bin_count, dtype=np.int64)[:, None]
    shifts = np.arange(lag_count, dtype=np.int64)[None, :] - maxlag
    phase_angle = (freq_index * shifts % samples).astype(np.float32) * np.float32(
        2.0 * math.pi / samples
    )
    phase_angle = phase_angle.astype(np.float64)
    weight = np.where(freq_index == 0, 1.0, 2.0).astype(np.float32) / np.float32(
        2.0 * math.sqrt(bin_count)
    )
    table = np.stack([np.cos(phase_angle), -np.sin(phase_angle)], axis=0)
    table = weight[None] * table.astype(np.float32)
    return table.astype(ml_dtypes.bfloat16)


def kernel(
    sensor_n, band_n, win_n, item_count,
    records, alive_hbm, basis_hbm, lag_hbm, out,
    alive, basis, lag, rows_in, outgoing, spread, wide, turned, totals, stacked, sending, homed,
    table_sem, own_sem, near_sem, far_sem, send1, recv1, send2, recv2, send3, recv3,
):
    z, b, c = lax.axis_index("sensor"), lax.axis_index("band"), lax.axis_index("win")
    groups = band_n * win_n
    g = b * win_n + c
    me = z * groups + g
    rows, samples = rows_in.shape
    part = samples // groups
    shard = alive.shape[0]
    half = LANES // 2
    local_items = item_count // groups
    ends = [sum(CHUNKS[: turn + 1]) * shard for turn in range(len(CHUNKS))]
    chunks = [(end - windows * shard, windows * shard) for end, windows in zip(ends, CHUNKS)]

    offsets = [
        (dz, db, dc) for dz in range(sensor_n) for db in range(band_n) for dc in range(win_n)
    ]

    z_high, z_low = lax.div(z, 2), lax.rem(z, 2)

    def peer(dz, db, dc):
        return (
            2 * lax.rem(z_high + dz // 2, 2) + lax.rem(z_low + dz % 2, 2),
            lax.rem(b + db, band_n),
            lax.rem(c + dc, win_n),
        )

    def ident(place):
        return {"sensor": place[0], "band": place[1], "win": place[2]}

    alive_copy = pltpu.make_async_copy(alive_hbm, alive, table_sem.at[2])
    alive_copy.start()
    basis_copy = pltpu.make_async_copy(basis_hbm, basis, table_sem.at[0])
    lag_copy = pltpu.make_async_copy(lag_hbm, lag, table_sem.at[1])

    def mine_of(group, start, count):
        return records.at[pl.ds(pl.multiple_of(group * rows + start, 16), count)]

    def columns_of(group, start, count):
        columns = pl.ds(pl.multiple_of(group * part, LANES), part)
        return rows_in.at[start : start + count, columns]

    own_copy = pltpu.make_async_copy(mine_of(g, 0, rows), columns_of(g, 0, rows), own_sem.at[0])
    own_copy.start()

    mate = ident(peer(0, 0, 1))
    first, second = c == 0, c == 1
    barrier = pltpu.get_barrier_semaphore()
    for off in offsets[1:]:
        place = peer(*off)

        @pl.when(place[2] == (0 if off[0] == 0 else 1))
        def _(place=place):
            pl.semaphore_signal(barrier, inc=1, device_id=ident(place), device_id_type=MESH)

    basis_copy.start()

    @pl.when(first)
    def _():
        pl.semaphore_wait(barrier, groups - 1)
        pl.semaphore_signal(near_sem, inc=1, device_id=mate, device_id_type=MESH)

    @pl.when(second)
    def _():
        pl.semaphore_wait(near_sem, 1)

    copies1 = {}
    for turn, (start, count) in enumerate(chunks):
        for db in reversed(range(band_n)):
            for dc in range(win_n):
                if (db, dc) == (0, 0):
                    continue
                slot = turn * groups + db * win_n + dc
                place = peer(0, db, dc)
                copy = pltpu.make_async_remote_copy(
                    src_ref=mine_of(place[1] * win_n + place[2], start, count),
                    dst_ref=columns_of(g, start, count),
                    send_sem=send1.at[slot],
                    recv_sem=recv1.at[slot],
                    device_id=ident(place),
                    device_id_type=MESH,
                )
                copy.start()
                copies1[turn, db, dc] = copy
    lag_copy.start()

    alive_copy.wait()
    row_item = lax.broadcasted_iota(jnp.int32, (rows, item_count), 0) // shard
    item = lax.broadcasted_iota(jnp.int32, (rows, item_count), 1)
    pick = jnp.where(row_item + g * local_items == item, 1.0, 0.0)
    spread_alive = lax.dot_general(
        pick.astype(jnp.bfloat16),
        alive[...].astype(jnp.float32).astype(jnp.bfloat16),
        (((1,), (1,)), ((), ())),
        preferred_element_type=jnp.float32,
    )
    row_sensor = lax.rem(lax.broadcasted_iota(jnp.int32, (rows, shard), 0), shard)
    column = lax.broadcasted_iota(jnp.int32, (rows, shard), 1)
    usable = jnp.sum(
        jnp.where(row_sensor == column, spread_alive, 0.0), axis=1, keepdims=True
    )

    own_copy.wait()
    basis_copy.wait()

    @pl.when(second)
    def _():
        pl.semaphore_wait(barrier, (sensor_n - 1) * groups)
        pl.semaphore_signal(far_sem, inc=1, device_id=mate, device_id_type=MESH)

    @pl.when(first)
    def _():
        pl.semaphore_wait(far_sem, 1)

    copies2 = {}
    order = [(dz, db) for near in ((2, 3), (1, 0)) for db in (1, 0) for dz in near]
    for turn, (start, count) in enumerate(chunks):
        lines = slice(start, start + count)
        for (at, _, _), copy in copies1.items():
            if at == turn:
                copy.wait_recv()
        if turn == len(chunks) - 1:
            order = [(dz, db) for db in (1, 0) for dz in (2, 1, 3, 0)]
        for step, (dz, db) in enumerate(order):
            place_z, place_b, _ = peer(dz, db, 0)
            spectra = jnp.dot(
                rows_in[lines, :],
                basis[place_z * band_n + place_b],
                preferred_element_type=jnp.float32,
            )
            for core in range(win_n):
                piece = spectra[:, core * LANES : (core + 1) * LANES]
                square = piece * piece
                power = square + pltpu.roll(square, half, 1)
                white = piece * (lax.rsqrt(power + WHITEN_FLOOR) * usable[lines])
                outgoing[step, core, lines] = white.astype(jnp.bfloat16)
            for dc in range(win_n):
                place = peer(dz, db, dc)
                if (dz, db, dc) == (0, 0, 0):
                    spread[me, lines, :] = outgoing[step, c, lines]
                    continue
                slot = ((turn * sensor_n + dz) * band_n + db) * win_n + dc
                copy = pltpu.make_async_remote_copy(
                    src_ref=outgoing.at[step, place[2], lines],
                    dst_ref=spread.at[me, lines],
                    send_sem=send2.at[slot],
                    recv_sem=recv2.at[slot],
                    device_id=ident(place),
                    device_id_type=MESH,
                )
                copy.start()
                copies2[turn, dz, db, dc] = copy

    def send_home(home_z, home_g):
        to = home_z * groups + home_g
        block = stacked[to].astype(jnp.bfloat16)
        sending[to] = block

        @pl.when(me == to)
        def _():
            homed[me] = sending[to]

        @pl.when(me != to)
        def _():
            pltpu.make_async_remote_copy(
                src_ref=sending.at[to],
                dst_ref=homed.at[me],
                send_sem=send3.at[to],
                recv_sem=recv3.at[me],
                device_id=ident((home_z, home_g // win_n, home_g % win_n)),
                device_id_type=MESH,
            ).start()

    lane = lax.broadcasted_iota(jnp.int32, (shard, LANES), 1)
    window_scale = 1.0 / math.sqrt(item_count)
    near = [(db, dc) for db in (1, 0) for dc in range(win_n)]
    waves = [
        (turn, near[at : at + groups // splits])
        for turn, splits in enumerate(SPLITS)
        for at in range(0, groups, groups // splits)
    ]
    for stage, (turn, sources) in enumerate(waves):
        start, count = chunks[turn]
        lines = slice(start, start + count)
        step_items = count // shard
        for db, dc in sources:
            for dz in range(sensor_n):
                if (dz, db, dc) != (0, 0, 0):
                    copies2[turn, dz, db, dc].wait_recv()
        for k, (db, dc) in enumerate(sources):
            _, source_b, source_c = peer(0, db, dc)
            source_g = source_b * win_n + source_c
            items = slice(k * step_items, (k + 1) * step_items)
            for source_z in range(sensor_n):
                block = spread[source_z * groups + source_g, lines, :].astype(jnp.float32)
                wide[source_z, items] = block.reshape(step_items, shard, LANES)
                turned[source_z, items] = pltpu.roll(block, half, 1).reshape(
                    step_items, shard, LANES
                )

        for first_z in range(sensor_n):
            seconds = list(range(first_z, sensor_n))
            batch = 4 if len(seconds) > 2 else 8
            for begin in range(0, shard, batch):
                places = [
                    (second_z, part, begin + k)
                    for second_z in seconds
                    for k in range(batch)
                    for part in range(2)
                ]

                def add(w, sums, first_z=first_z, begin=begin, batch=batch, places=places):
                    left = [
                        jnp.broadcast_to(wide[first_z, w, s : s + 1, :], (shard, LANES))
                        for s in range(begin, begin + batch)
                    ]
                    right = {
                        (z2, part): (turned if part else wide)[z2, w]
                        for z2 in range(first_z, sensor_n)
                        for part in range(2)
                    }
                    return tuple(
                        total + left[s - begin] * right[z2, part]
                        for total, (z2, part, s) in zip(sums, places, strict=True)
                    )

                if stage == 0:
                    first_sums = (jnp.zeros((shard, LANES), jnp.float32),) * len(places)
                else:
                    first_sums = tuple(
                        totals[first_z * sensor_n + z2, part, s] for z2, part, s in places
                    )
                sums = lax.fori_loop(
                    0, len(sources) * step_items, add, first_sums, unroll=UNROLL
                )
                if stage < len(waves) - 1:
                    for total, (z2, part, s) in zip(sums, places, strict=True):
                        totals[first_z * sensor_n + z2, part, s] = total
                    continue
                found = dict(zip(places, sums, strict=True))
                for z2 in seconds:
                    for s in range(begin, begin + batch):
                        same, cross = found[z2, 0, s], found[z2, 1, s]
                        real = (same + pltpu.roll(same, half, 1)) * window_scale
                        imag = (cross - pltpu.roll(cross, half, 1)) * window_scale
                        stacked[first_z * groups + z2, s * shard : (s + 1) * shard, :] = jnp.where(
                            lane < half, real, imag
                        )
                        if z2 != first_z:
                            stacked[z2 * groups + first_z, pl.ds(s, shard, stride=shard), :] = (
                                jnp.where(lane < half, real, -imag)
                            )
            if stage == len(waves) - 1:
                for home_z, home_g in [(first_z, z2) for z2 in seconds] + [
                    (z2, first_z) for z2 in seconds[1:]
                ]:
                    send_home(home_z, home_g)
    lag_copy.wait()
    lagged = None
    for near in range(sensor_n):
        for dz, db, dc in offsets:
            if dz == near and (dz, db, dc) != (0, 0, 0):
                place = peer(dz, db, dc)
                source = place[0] * groups + place[1] * win_n + place[2]
                pltpu.make_async_remote_copy(
                    src_ref=sending.at[source],
                    dst_ref=homed.at[source],
                    send_sem=send3.at[source],
                    recv_sem=recv3.at[source],
                    device_id=ident(place),
                    device_id_type=MESH,
                ).wait_recv()
        first_source = peer(near, 0, 0)[0] * groups
        block = jnp.concatenate([homed[first_source + at] for at in range(groups)], axis=1)
        depth = groups * LANES
        term = jnp.dot(
            block,
            lag[pl.ds(pl.multiple_of(first_source * LANES, depth), depth)],
            preferred_element_type=jnp.float32,
        )
        lagged = term if lagged is None else lagged + term
    out[...] = lagged[:, : out.shape[1]]
    for copy in [*copies1.values(), *copies2.values()]:
        copy.wait_send()
    for off in offsets[1:]:
        place = peer(*off)
        to = place[0] * groups + place[1] * win_n + place[2]
        pltpu.make_async_remote_copy(
            src_ref=sending.at[to],
            dst_ref=homed.at[me],
            send_sem=send3.at[to],
            recv_sem=recv3.at[to],
            device_id=ident(place),
            device_id_type=MESH,
        ).wait_send()


def fused(sizes, records, alive):
    sensor_n, band_n, win_n = sizes
    groups = band_n * win_n
    peers = sensor_n * groups
    item_count, shard, part = records.shape
    samples = part * groups
    bin_count = samples // 2
    half = LANES // 2
    rows = item_count // groups * shard
    lag_count = 2 * MAXLAG + 1
    stage_items = max(groups // cut * windows for windows, cut in zip(CHUNKS, SPLITS))
    lag_room = -(-lag_count // LANES) * LANES
    table = spectrum_table(samples, bin_count).reshape(samples, 2, peers, half)
    table = table.transpose(0, 2, 1, 3).reshape(samples, peers // win_n, win_n * LANES)
    basis = np.ascontiguousarray(table.transpose(1, 0, 2))
    table = lag_table(samples, bin_count, MAXLAG).reshape(2, peers, half, lag_count)
    table = table.transpose(1, 0, 2, 3).reshape(2 * bin_count, lag_count)
    lag = np.zeros((2 * bin_count, lag_room), ml_dtypes.bfloat16)
    lag[:, :lag_count] = table
    vmem = pl.BlockSpec(memory_space=pltpu.VMEM)
    far = pl.BlockSpec(memory_space=pltpu.HBM)
    dma = pltpu.SemaphoreType.DMA
    result = pl.pallas_call(
        functools.partial(kernel, sensor_n, band_n, win_n, item_count),
        out_shape=pltpu.VMEM((shard * shard, lag_count), jnp.float32),
        in_specs=[far, far, far, far],
        out_specs=vmem,
        scratch_shapes=[
            pltpu.VMEM((shard, item_count), jnp.int32),
            pltpu.VMEM(basis.shape, jnp.bfloat16),
            pltpu.VMEM(lag.shape, jnp.bfloat16),
            pltpu.VMEM((rows, samples), jnp.bfloat16),
            pltpu.VMEM((peers // win_n, win_n, rows, LANES), jnp.bfloat16),
            pltpu.VMEM((peers, rows, LANES), jnp.bfloat16),
            pltpu.VMEM((sensor_n, stage_items, shard, LANES), jnp.float32),
            pltpu.VMEM((sensor_n, stage_items, shard, LANES), jnp.float32),
            pltpu.VMEM((peers, 2, shard, shard, LANES), jnp.float32),
            pltpu.VMEM((peers, shard * shard, LANES), jnp.float32),
            pltpu.VMEM((peers, shard * shard, LANES), jnp.bfloat16),
            pltpu.VMEM((peers, shard * shard, LANES), jnp.bfloat16),
            dma((3,)),
            dma((2,)),
            pltpu.SemaphoreType.REGULAR,
            pltpu.SemaphoreType.REGULAR,
            dma((len(CHUNKS) * groups,)),
            dma((len(CHUNKS) * groups,)),
            dma((len(CHUNKS) * peers,)),
            dma((len(CHUNKS) * peers,)),
            dma((peers,)),
            dma((peers,)),
        ],
        compiler_params=pltpu.CompilerParams(
            collective_id=0, has_side_effects=True, vmem_limit_bytes=56 << 20
        ),
    )(
        records.reshape(item_count * shard, part),
        alive.T,
        jnp.asarray(basis),
        jnp.asarray(lag),
    )
    return result.reshape(shard, shard, lag_count)


def cross_block(local_spec, incoming, window_scale):
    products = jnp.einsum(
        "wicf,nwjdf->injcdf", local_spec, incoming, preferred_element_type=jnp.float32
    )
    real_part = products[:, :, :, 0, 0] + products[:, :, :, 1, 1]
    imag_part = products[:, :, :, 1, 0] - products[:, :, :, 0, 1]
    return jnp.stack([real_part, imag_part], axis=3) * window_scale


def general(records, alive):
    groups = lax.axis_size(ROW_AXES)
    sensors_count = lax.axis_size("sensor")
    shard_sensors = records.shape[1]
    samples = records.shape[2] * groups
    bin_count = samples // 2
    bins_local = bin_count // groups
    dft_basis = jnp.asarray(spectrum_table(samples, bin_count).reshape(samples, -1))
    pieces = lax.all_to_all(records, ROW_AXES, split_axis=1, concat_axis=2, tiled=True)
    item_count = pieces.shape[0]
    sample_rows = pieces.reshape(-1, samples)
    spectra = jnp.dot(sample_rows, dft_basis, preferred_element_type=jnp.float32)
    spectra = spectra.reshape(item_count, -1, 2, bin_count)
    power_sum = spectra[:, :, 0] * spectra[:, :, 0] + spectra[:, :, 1] * spectra[:, :, 1]
    whitened = (spectra * lax.rsqrt(power_sum + WHITEN_FLOOR)[:, :, None, :]).astype(jnp.bfloat16)
    spectra = lax.all_to_all(whitened, ROW_AXES, split_axis=3, concat_axis=1, tiled=True)
    spectra = spectra * alive.astype(jnp.bfloat16)[:, :, None, None]
    window_scale = 1.0 / math.sqrt(spectra.shape[0])
    spread = lax.all_to_all(spectra, "sensor", split_axis=3, concat_axis=1, tiled=True)
    every_pair = cross_block(spread, spread[None], window_scale)[:, 0]
    paired = every_pair.astype(jnp.bfloat16)
    homed = lax.all_to_all(paired, "sensor", split_axis=0, concat_axis=3, tiled=True)
    stacked = homed.reshape(shard_sensors, sensors_count, shard_sensors, 2, bins_local)
    relaid = lax.all_to_all(stacked, ROW_AXES, split_axis=1, concat_axis=4, tiled=True)
    flattened = relaid.reshape(-1, 2 * bin_count)
    lag_basis = jnp.asarray(lag_table(samples, bin_count, MAXLAG).reshape(2 * bin_count, -1))
    lagged = jnp.dot(flattened, lag_basis, preferred_element_type=jnp.float32)
    return lagged.reshape(shard_sensors, -1, 2 * MAXLAG + 1)


def body(sizes, records, alive):
    sensor_n, band_n, win_n = sizes
    groups = band_n * win_n
    item_count, shard, part = records.shape
    fits = (
        part * groups == sensor_n * groups * LANES
        and (sensor_n, band_n, win_n) == (4, 2, 2)
        and shard == 8
        and item_count == groups * sum(CHUNKS)
        and part % LANES == 0
    )
    if fits:
        return fused(sizes, records, alive)
    return general(records, alive)


def solution(mesh):
    sizes = tuple(mesh.shape[name] for name in ("sensor", "band", "win"))
    return jax.shard_map(
        functools.partial(body, sizes),
        mesh=mesh,
        in_specs=(P("days", "sensor", ROW_AXES), P("days", "sensor")),
        out_specs=P(("days", "sensor"), ROW_AXES, None),
        check_vma=False,
    )
```

```python
import functools
import math

import jax
import jax.numpy as jnp
import ml_dtypes
import numpy as np
from jax import lax
from jax.experimental import pallas as pl
from jax.experimental.pallas import tpu as pltpu
from jax.sharding import PartitionSpec as P

MAXLAG = 300
WHITEN_FLOOR = 0.5
LANES = 128
UNROLL = 4
CHUNKS = (6, 8, 10)
SPLITS = (1, 1, 2)
ROW_AXES = ("band", "win")
MESH = pl.DeviceIdType.MESH


def spectrum_table(samples, bin_count):
    time_index = np.arange(samples, dtype=np.int64)[:, None]
    freq_index = np.arange(bin_count, dtype=np.int64)[None, :]
    phase_angle = (time_index * freq_index % samples).astype(np.float32) * np.float32(
        2.0 * math.pi / samples
    )
    phase_angle = phase_angle.astype(np.float64)
    table = np.stack([np.cos(phase_angle), -np.sin(phase_angle)], axis=1)
    table = table.astype(np.float32) / np.float32(math.sqrt(samples))
    return table.astype(ml_dtypes.bfloat16)


def lag_table(samples, bin_count, maxlag):
    lag_count = 2 * maxlag + 1
    freq_index = np.arange(bin_count, dtype=np.int64)[:, None]
    shifts = np.arange(lag_count, dtype=np.int64)[None, :] - maxlag
    phase_angle = (freq_index * shifts % samples).astype(np.float32) * np.float32(
        2.0 * math.pi / samples
    )
    phase_angle = phase_angle.astype(np.float64)
    weight = np.where(freq_index == 0, 1.0, 2.0).astype(np.float32) / np.float32(
        2.0 * math.sqrt(bin_count)
    )
    table = np.stack([np.cos(phase_angle), -np.sin(phase_angle)], axis=0)
    table = weight[None] * table.astype(np.float32)
    return table.astype(ml_dtypes.bfloat16)


def kernel(
    sensor_n, band_n, win_n, item_count,
    records, alive_hbm, basis_hbm, lag_hbm, out,
    alive, basis, lag, rows_in, outgoing, spread, wide, turned, totals, stacked, sending, homed,
    table_sem, own_sem, near_sem, far_sem, send1, recv1, send2, recv2, send3, recv3,
):
    z, b, c = lax.axis_index("sensor"), lax.axis_index("band"), lax.axis_index("win")
    groups = band_n * win_n
    g = b * win_n + c
    me = z * groups + g
    rows, samples = rows_in.shape
    part = samples // groups
    shard = alive.shape[0]
    half = LANES // 2
    local_items = item_count // groups
    ends = [sum(CHUNKS[: turn + 1]) * shard for turn in range(len(CHUNKS))]
    chunks = [(end - windows * shard, windows * shard) for end, windows in zip(ends, CHUNKS)]

    offsets = [
        (dz, db, dc) for dz in range(sensor_n) for db in range(band_n) for dc in range(win_n)
    ]

    z_high, z_low = lax.div(z, 2), lax.rem(z, 2)

    def peer(dz, db, dc):
        return (
            2 * lax.rem(z_high + dz // 2, 2) + lax.rem(z_low + dz % 2, 2),
            lax.rem(b + db, band_n),
            lax.rem(c + dc, win_n),
        )

    def ident(place):
        return {"sensor": place[0], "band": place[1], "win": place[2]}

    alive_copy = pltpu.make_async_copy(alive_hbm, alive, table_sem.at[2])
    alive_copy.start()
    basis_copy = pltpu.make_async_copy(basis_hbm, basis, table_sem.at[0])
    lag_copy = pltpu.make_async_copy(lag_hbm, lag, table_sem.at[1])

    def mine_of(group, start, count):
        return records.at[pl.ds(pl.multiple_of(group * rows + start, 16), count)]

    def columns_of(group, start, count):
        columns = pl.ds(pl.multiple_of(group * part, LANES), part)
        return rows_in.at[start : start + count, columns]

    own_copy = pltpu.make_async_copy(mine_of(g, 0, rows), columns_of(g, 0, rows), own_sem.at[0])
    own_copy.start()

    mate = ident(peer(0, 0, 1))
    first, second = c == 0, c == 1
    barrier = pltpu.get_barrier_semaphore()
    for off in offsets[1:]:
        place = peer(*off)

        @pl.when(place[2] == (0 if off[0] == 0 else 1))
        def _(place=place):
            pl.semaphore_signal(barrier, inc=1, device_id=ident(place), device_id_type=MESH)

    basis_copy.start()

    @pl.when(first)
    def _():
        pl.semaphore_wait(barrier, groups - 1)
        pl.semaphore_signal(near_sem, inc=1, device_id=mate, device_id_type=MESH)

    @pl.when(second)
    def _():
        pl.semaphore_wait(near_sem, 1)

    copies1 = {}
    for turn, (start, count) in enumerate(chunks):
        for db in reversed(range(band_n)):
            for dc in range(win_n):
                if (db, dc) == (0, 0):
                    continue
                slot = turn * groups + db * win_n + dc
                place = peer(0, db, dc)
                copy = pltpu.make_async_remote_copy(
                    src_ref=mine_of(place[1] * win_n + place[2], start, count),
                    dst_ref=columns_of(g, start, count),
                    send_sem=send1.at[slot],
                    recv_sem=recv1.at[slot],
                    device_id=ident(place),
                    device_id_type=MESH,
                )
                copy.start()
                copies1[turn, db, dc] = copy
    lag_copy.start()

    alive_copy.wait()
    row_item = lax.broadcasted_iota(jnp.int32, (rows, item_count), 0) // shard
    item = lax.broadcasted_iota(jnp.int32, (rows, item_count), 1)
    pick = jnp.where(row_item + g * local_items == item, 1.0, 0.0)
    spread_alive = lax.dot_general(
        pick.astype(jnp.bfloat16),
        alive[...].astype(jnp.float32).astype(jnp.bfloat16),
        (((1,), (1,)), ((), ())),
        preferred_element_type=jnp.float32,
    )
    row_sensor = lax.rem(lax.broadcasted_iota(jnp.int32, (rows, shard), 0), shard)
    column = lax.broadcasted_iota(jnp.int32, (rows, shard), 1)
    usable = jnp.sum(
        jnp.where(row_sensor == column, spread_alive, 0.0), axis=1, keepdims=True
    )

    own_copy.wait()
    basis_copy.wait()

    @pl.when(second)
    def _():
        pl.semaphore_wait(barrier, (sensor_n - 1) * groups)
        pl.semaphore_signal(far_sem, inc=1, device_id=mate, device_id_type=MESH)

    @pl.when(first)
    def _():
        pl.semaphore_wait(far_sem, 1)

    copies2 = {}
    order = [(dz, db) for near in ((2, 3), (1, 0)) for db in (1, 0) for dz in near]
    for turn, (start, count) in enumerate(chunks):
        lines = slice(start, start + count)
        for (at, _, _), copy in copies1.items():
            if at == turn:
                copy.wait_recv()
        if turn == len(chunks) - 1:
            order = [(dz, db) for db in (1, 0) for dz in (2, 1, 3, 0)]
        for step, (dz, db) in enumerate(order):
            place_z, place_b, _ = peer(dz, db, 0)
            spectra = jnp.dot(
                rows_in[lines, :],
                basis[place_z * band_n + place_b],
                preferred_element_type=jnp.float32,
            )
            for core in range(win_n):
                piece = spectra[:, core * LANES : (core + 1) * LANES]
                square = piece * piece
                power = square + pltpu.roll(square, half, 1)
                white = piece * (lax.rsqrt(power + WHITEN_FLOOR) * usable[lines])
                outgoing[step, core, lines] = white.astype(jnp.bfloat16)
            for dc in range(win_n):
                place = peer(dz, db, dc)
                if (dz, db, dc) == (0, 0, 0):
                    spread[me, lines, :] = outgoing[step, c, lines]
                    continue
                slot = ((turn * sensor_n + dz) * band_n + db) * win_n + dc
                copy = pltpu.make_async_remote_copy(
                    src_ref=outgoing.at[step, place[2], lines],
                    dst_ref=spread.at[me, lines],
                    send_sem=send2.at[slot],
                    recv_sem=recv2.at[slot],
                    device_id=ident(place),
                    device_id_type=MESH,
                )
                copy.start()
                copies2[turn, dz, db, dc] = copy

    def send_home(home_z, home_g):
        to = home_z * groups + home_g
        block = stacked[to].astype(jnp.bfloat16)
        sending[to] = block

        @pl.when(me == to)
        def _():
            homed[me] = sending[to]

        @pl.when(me != to)
        def _():
            pltpu.make_async_remote_copy(
                src_ref=sending.at[to],
                dst_ref=homed.at[me],
                send_sem=send3.at[to],
                recv_sem=recv3.at[me],
                device_id=ident((home_z, home_g // win_n, home_g % win_n)),
                device_id_type=MESH,
            ).start()

    lane = lax.broadcasted_iota(jnp.int32, (shard, LANES), 1)
    window_scale = 1.0 / math.sqrt(item_count)
    near = [(db, dc) for db in (1, 0) for dc in range(win_n)]
    waves = [
        (turn, near[at : at + groups // splits])
        for turn, splits in enumerate(SPLITS)
        for at in range(0, groups, groups // splits)
    ]
    for stage, (turn, sources) in enumerate(waves):
        start, count = chunks[turn]
        lines = slice(start, start + count)
        step_items = count // shard
        for db, dc in sources:
            for dz in range(sensor_n):
                if (dz, db, dc) != (0, 0, 0):
                    copies2[turn, dz, db, dc].wait_recv()
        for k, (db, dc) in enumerate(sources):
            _, source_b, source_c = peer(0, db, dc)
            source_g = source_b * win_n + source_c
            items = slice(k * step_items, (k + 1) * step_items)
            for source_z in range(sensor_n):
                block = spread[source_z * groups + source_g, lines, :].astype(jnp.float32)
                wide[source_z, items] = block.reshape(step_items, shard, LANES)
                turned[source_z, items] = pltpu.roll(block, half, 1).reshape(
                    step_items, shard, LANES
                )

        for first_z in range(sensor_n):
            seconds = list(range(first_z, sensor_n))
            batch = 4 if len(seconds) > 2 else 8
            for begin in range(0, shard, batch):
                places = [
                    (second_z, part, begin + k)
                    for second_z in seconds
                    for k in range(batch)
                    for part in range(2)
                ]

                def add(w, sums, first_z=first_z, begin=begin, batch=batch, places=places):
                    left = [
                        jnp.broadcast_to(wide[first_z, w, s : s + 1, :], (shard, LANES))
                        for s in range(begin, begin + batch)
                    ]
                    right = {
                        (z2, part): (turned if part else wide)[z2, w]
                        for z2 in range(first_z, sensor_n)
                        for part in range(2)
                    }
                    return tuple(
                        total + left[s - begin] * right[z2, part]
                        for total, (z2, part, s) in zip(sums, places, strict=True)
                    )

                if stage == 0:
                    first_sums = (jnp.zeros((shard, LANES), jnp.float32),) * len(places)
                else:
                    first_sums = tuple(
                        totals[first_z * sensor_n + z2, part, s] for z2, part, s in places
                    )
                sums = lax.fori_loop(
                    0, len(sources) * step_items, add, first_sums, unroll=UNROLL
                )
                if stage < len(waves) - 1:
                    for total, (z2, part, s) in zip(sums, places, strict=True):
                        totals[first_z * sensor_n + z2, part, s] = total
                    continue
                found = dict(zip(places, sums, strict=True))
                for z2 in seconds:
                    for s in range(begin, begin + batch):
                        same, cross = found[z2, 0, s], found[z2, 1, s]
                        real = (same + pltpu.roll(same, half, 1)) * window_scale
                        imag = (cross - pltpu.roll(cross, half, 1)) * window_scale
                        stacked[first_z * groups + z2, s * shard : (s + 1) * shard, :] = jnp.where(
                            lane < half, real, imag
                        )
                        if z2 != first_z:
                            stacked[z2 * groups + first_z, pl.ds(s, shard, stride=shard), :] = (
                                jnp.where(lane < half, real, -imag)
                            )
            if stage == len(waves) - 1:
                for home_z, home_g in [(first_z, z2) for z2 in seconds] + [
                    (z2, first_z) for z2 in seconds[1:]
                ]:
                    send_home(home_z, home_g)
    lag_copy.wait()
    lagged = None
    for near in range(sensor_n):
        for dz, db, dc in offsets:
            if dz == near and (dz, db, dc) != (0, 0, 0):
                place = peer(dz, db, dc)
                source = place[0] * groups + place[1] * win_n + place[2]
                pltpu.make_async_remote_copy(
                    src_ref=sending.at[source],
                    dst_ref=homed.at[source],
                    send_sem=send3.at[source],
                    recv_sem=recv3.at[source],
                    device_id=ident(place),
                    device_id_type=MESH,
                ).wait_recv()
        first_source = peer(near, 0, 0)[0] * groups
        block = jnp.concatenate([homed[first_source + at] for at in range(groups)], axis=1)
        depth = groups * LANES
        term = jnp.dot(
            block,
            lag[pl.ds(pl.multiple_of(first_source * LANES, depth), depth)],
            preferred_element_type=jnp.float32,
        )
        lagged = term if lagged is None else lagged + term
    out[...] = lagged[:, : out.shape[1]]
    for copy in [*copies1.values(), *copies2.values()]:
        copy.wait_send()
    for off in offsets[1:]:
        place = peer(*off)
        to = place[0] * groups + place[1] * win_n + place[2]
        pltpu.make_async_remote_copy(
            src_ref=sending.at[to],
            dst_ref=homed.at[me],
            send_sem=send3.at[to],
            recv_sem=recv3.at[to],
            device_id=ident(place),
            device_id_type=MESH,
        ).wait_send()


def fused(sizes, records, alive):
    sensor_n, band_n, win_n = sizes
    groups = band_n * win_n
    peers = sensor_n * groups
    item_count, shard, part = records.shape
    samples = part * groups
    bin_count = samples // 2
    half = LANES // 2
    rows = item_count // groups * shard
    lag_count = 2 * MAXLAG + 1
    stage_items = max(groups // cut * windows for windows, cut in zip(CHUNKS, SPLITS))
    lag_room = -(-lag_count // LANES) * LANES
    table = spectrum_table(samples, bin_count).reshape(samples, 2, peers, half)
    table = table.transpose(0, 2, 1, 3).reshape(samples, peers // win_n, win_n * LANES)
    basis = np.ascontiguousarray(table.transpose(1, 0, 2))
    table = lag_table(samples, bin_count, MAXLAG).reshape(2, peers, half, lag_count)
    table = table.transpose(1, 0, 2, 3).reshape(2 * bin_count, lag_count)
    lag = np.zeros((2 * bin_count, lag_room), ml_dtypes.bfloat16)
    lag[:, :lag_count] = table
    vmem = pl.BlockSpec(memory_space=pltpu.VMEM)
    far = pl.BlockSpec(memory_space=pltpu.HBM)
    dma = pltpu.SemaphoreType.DMA
    result = pl.pallas_call(
        functools.partial(kernel, sensor_n, band_n, win_n, item_count),
        out_shape=pltpu.VMEM((shard * shard, lag_count), jnp.float32),
        in_specs=[far, far, far, far],
        out_specs=vmem,
        scratch_shapes=[
            pltpu.VMEM((shard, item_count), jnp.int32),
            pltpu.VMEM(basis.shape, jnp.bfloat16),
            pltpu.VMEM(lag.shape, jnp.bfloat16),
            pltpu.VMEM((rows, samples), jnp.bfloat16),
            pltpu.VMEM((peers // win_n, win_n, rows, LANES), jnp.bfloat16),
            pltpu.VMEM((peers, rows, LANES), jnp.bfloat16),
            pltpu.VMEM((sensor_n, stage_items, shard, LANES), jnp.float32),
            pltpu.VMEM((sensor_n, stage_items, shard, LANES), jnp.float32),
            pltpu.VMEM((peers, 2, shard, shard, LANES), jnp.float32),
            pltpu.VMEM((peers, shard * shard, LANES), jnp.float32),
            pltpu.VMEM((peers, shard * shard, LANES), jnp.bfloat16),
            pltpu.VMEM((peers, shard * shard, LANES), jnp.bfloat16),
            dma((3,)),
            dma((2,)),
            pltpu.SemaphoreType.REGULAR,
            pltpu.SemaphoreType.REGULAR,
            dma((len(CHUNKS) * groups,)),
            dma((len(CHUNKS) * groups,)),
            dma((len(CHUNKS) * peers,)),
            dma((len(CHUNKS) * peers,)),
            dma((peers,)),
            dma((peers,)),
        ],
        compiler_params=pltpu.CompilerParams(
            collective_id=0, has_side_effects=True, vmem_limit_bytes=56 << 20
        ),
    )(
        records.reshape(item_count * shard, part),
        alive.T,
        jnp.asarray(basis),
        jnp.asarray(lag),
    )
    return result.reshape(shard, shard, lag_count)


def cross_block(local_spec, incoming, window_scale):
    products = jnp.einsum(
        "wicf,nwjdf->injcdf", local_spec, incoming, preferred_element_type=jnp.float32
    )
    real_part = products[:, :, :, 0, 0] + products[:, :, :, 1, 1]
    imag_part = products[:, :, :, 1, 0] - products[:, :, :, 0, 1]
    return jnp.stack([real_part, imag_part], axis=3) * window_scale


def general(records, alive):
    groups = lax.axis_size(ROW_AXES)
    sensors_count = lax.axis_size("sensor")
    shard_sensors = records.shape[1]
    samples = records.shape[2] * groups
    bin_count = samples // 2
    bins_local = bin_count // groups
    dft_basis = jnp.asarray(spectrum_table(samples, bin_count).reshape(samples, -1))
    pieces = lax.all_to_all(records, ROW_AXES, split_axis=1, concat_axis=2, tiled=True)
    item_count = pieces.shape[0]
    sample_rows = pieces.reshape(-1, samples)
    spectra = jnp.dot(sample_rows, dft_basis, preferred_element_type=jnp.float32)
    spectra = spectra.reshape(item_count, -1, 2, bin_count)
    power_sum = spectra[:, :, 0] * spectra[:, :, 0] + spectra[:, :, 1] * spectra[:, :, 1]
    whitened = (spectra * lax.rsqrt(power_sum + WHITEN_FLOOR)[:, :, None, :]).astype(jnp.bfloat16)
    spectra = lax.all_to_all(whitened, ROW_AXES, split_axis=3, concat_axis=1, tiled=True)
    spectra = spectra * alive.astype(jnp.bfloat16)[:, :, None, None]
    window_scale = 1.0 / math.sqrt(spectra.shape[0])
    spread = lax.all_to_all(spectra, "sensor", split_axis=3, concat_axis=1, tiled=True)
    every_pair = cross_block(spread, spread[None], window_scale)[:, 0]
    paired = every_pair.astype(jnp.bfloat16)
    homed = lax.all_to_all(paired, "sensor", split_axis=0, concat_axis=3, tiled=True)
    stacked = homed.reshape(shard_sensors, sensors_count, shard_sensors, 2, bins_local)
    relaid = lax.all_to_all(stacked, ROW_AXES, split_axis=1, concat_axis=4, tiled=True)
    flattened = relaid.reshape(-1, 2 * bin_count)
    lag_basis = jnp.asarray(lag_table(samples, bin_count, MAXLAG).reshape(2 * bin_count, -1))
    lagged = jnp.dot(flattened, lag_basis, preferred_element_type=jnp.float32)
    return lagged.reshape(shard_sensors, -1, 2 * MAXLAG + 1)


def body(sizes, records, alive):
    sensor_n, band_n, win_n = sizes
    groups = band_n * win_n
    item_count, shard, part = records.shape
    fits = (
        part * groups == sensor_n * groups * LANES
        and (sensor_n, band_n, win_n) == (4, 2, 2)
        and shard == 8
        and item_count == groups * sum(CHUNKS)
        and part % LANES == 0
    )
    if fits:
        return fused(sizes, records, alive)
    return general(records, alive)


def solution(mesh):
    sizes = tuple(mesh.shape[name] for name in ("sensor", "band", "win"))
    return jax.shard_map(
        functools.partial(body, sizes),
        mesh=mesh,
        in_specs=(P("days", "sensor", ROW_AXES), P("days", "sensor")),
        out_specs=P(("days", "sensor"), ROW_AXES, None),
        check_vma=False,
    )
```
